512 devices in a mesh: mem: 4 (over x), lat: 4 (over y_hi, core), lon: 32 (over z, y_lo).
Axes of the slice: x: 4, y: 8 (y_hi: 2, y_lo: 4; y = y_hi * 4 + y_lo), z: 8, core: 2. Of those that a mesh axis runs over, the one named last changes fastest.
Arguments:
- initial_temp: float32 [100, 128, 512], P(None, 'lon', 'lat'), may hold values from -6 to 6
- land_mask: int32 [128, 512], P('lon', 'lat'), may hold values 0 or 1
- pert_table: float32 [16, 100], replicated, may hold values from 0.03 to 0.24
- pert_index: int32 [8], P('mem'), may hold values from 0 to 15
- base_kh: float32 [100], replicated, may hold values from 0.03 to 0.24
- member_mix: bfloat16 [8, 100, 100], P('mem'), may hold values from -0.15625 to 0.15625
- base_mix: bfloat16 [100, 100], replicated, may hold values from -0.15625 to 0.15625
- owner: int32 [32768, 1], P(('lat', 'lon')), may hold values from 0 to 127; in each aligned block of 256 rows (0 to 255, 256 to 511, ...) at most 4 rows name the same one
- column: int32 [32768], P(('lat', 'lon')), may hold values from 0 to 511
- interp_w: float32 [32768, 100], P(('lat', 'lon')), may hold values from 0 to 1
- obs_inv_var: float32 [32768, 100], P(('lat', 'lon')), may hold values from 1 to 16
- observed: float32 [32768, 100], P(('lat', 'lon')), may hold values from -6 to 6
Outputs:
- member_temp: bfloat16 [8, 100, 128, 512], P('mem', None, 'lon', 'lat')
- base_temp: bfloat16 [100, 128, 512], P(None, 'lon', 'lat')
- gram_block: float32 [8, 8], replicated
- projection: float32 [8], replicated
- misfit: float32 [32768, 100], P(('lat', 'lon'))
The draws below stay inside these ranges and needn't reach their ends.
Inputs may be any that keep to these rules, and one draw needn't show every extreme that they name: Within the records of one device no owner is named more than 4 times, and in every draw some owner is named exactly 4 times by some device's records. The column within the owner's block is the longitude offset times 128 plus the latitude offset.
All inputs are finite; a program needn't handle non-finite values. No bound on the sum of `land_mask` on one device may be relied on, other than what follows from the above.
Results may differ from the reference program's by a relative error of at most 0.012.
Values may be sent and summed in bfloat16 or wider, within the bound.
No kernel may reach another device: no remote copies, remote signals or barrier semaphores. Data moves between devices by JAX's collectives and lax.ppermute only.
A program may use at most 64 MiB of HBM per device.

```python
import math
import jax
import jax.numpy as jnp
import numpy as np
from jax import lax

K = 100
CX = 4
CY = 128
PROF_DEV = 256
STEPS = 5
NPERT = 16
MEMBERS = 8
LON = 128
LAT = 512
CAP = 4
PROFILES = 32768
N_LAT = 4
N_LON = 32


def touch_ends(entries, own_key, low, top_value):
    longest = entries.shape.index(max(entries.shape))
    spots = []
    for shift in (0, 1):
        where = [jax.random.randint(jax.random.fold_in(own_key, axis), (), 0, length) for axis, length in enumerate(entries.shape)]
        where[longest] = (where[longest] + shift) % entries.shape[longest]
        spots.append(tuple(where))
    return entries.at[spots[0]].set(low).at[spots[1]].set(top_value)


def shard_levels(stream_key, shape, shards, least, largest):
    factor_of = 1.0
    for position, shards_of in shards:
        heights = jax.random.uniform(jax.random.fold_in(jax.random.fold_in(stream_key, 6), position), (shards_of,), jnp.float32, least / len(shards), largest / len(shards))
        factor_of = factor_of * jnp.repeat(jnp.exp(heights), shape[position] // shards_of).reshape((-1,) + (1,) * (len(shape) - 1 - position))
    return factor_of


def deal_out(stream_key, own, number, rows, count, top, most, lean):
    sequence = jax.random.permutation(stream_key, count)
    heavy_load, ordinary = portions_of(count, rows * top, most, lean, True), portions_of(count, rows * top, most, lean, False)
    places = jnp.arange(count)

    def named(lengths, turn):
        used = int((lengths > 0).sum())
        fixed = max(1, used // 4)
        shifted = fixed + (places - fixed + turn * (used - fixed)) % max(1, count - fixed)
        return jnp.zeros((count,), jnp.int32).at[sequence[jnp.where(places < fixed, places, shifted)]].set(jnp.asarray(lengths, jnp.int32))

    lengths = jnp.where(number % 4 == 0, named(heavy_load, number // 4), named(ordinary, number - number // 4 - 1))
    mixed = jax.random.permutation(jax.random.fold_in(own, 3), count)
    source_of, taker = mixed[0:count // 2 * 2:2], mixed[1:count // 2 * 2:2]
    margin = jnp.minimum(lengths[source_of] - 1, most - lengths[taker]) // 2
    margin = jnp.where((source_of == sequence[0]) | (taker == sequence[0]) | (lengths[taker] == 0), 0, jnp.maximum(margin, 0))
    shifted = jax.random.randint(jax.random.fold_in(own, 4), (count // 2,), 0, 1 << 20) % (margin + 1)
    lengths = lengths.at[source_of].add(-shifted).at[taker].add(shifted)
    labels = jnp.searchsorted(jnp.cumsum(lengths), jnp.arange(rows * top), side="right").astype(jnp.int32)
    listing = labels.reshape(top, rows).T
    listing = listing[jax.random.permutation(jax.random.fold_in(own, 1), rows)]
    turn = jax.random.randint(jax.random.fold_in(own, 2), (rows, 1), 0, top)
    return jnp.take_along_axis(listing, (jnp.arange(top)[None, :] + turn) % top, axis=1)


def portions_of(amount, total, most, skew, full):
    loads = [(1 << 20) // math.isqrt(rank ** skew) + 1 for rank in range(1, amount + 1)]
    largest = most if full else min(most, max(-(-total // amount), total * loads[0] // sum(loads)))
    least = 1 if total - largest >= amount - 1 else 0
    given, surplus = [largest] + [least] * (amount - 1), total - largest - least * (amount - 1)
    while surplus > 0:
        candidates = [i for i in range(1, amount) if given[i] < largest] or [i for i in range(1, amount) if given[i] < most]
        mass, left = sum([loads[i] for i in candidates]), surplus
        for i in candidates:
            addition = min(most - given[i], max(1, left * loads[i] // mass), surplus)
            given[i] = given[i] + addition
            surplus = surplus - addition
    return np.array(given)


def noise(stream_key, extent, width, bound, split=(), dtype=jnp.bfloat16):
    drawn = width * jax.random.normal(stream_key, extent, jnp.float32)
    if split:
        drawn = drawn * shard_levels(stream_key, extent, split, -0.22, 0.18)
    return jnp.clip(drawn, -bound, bound).astype(dtype)


def setup_inputs(seed: int = 0) -> dict:
    arg_keys = jax.random.split(jax.random.key(seed), 13)
    initial_temp = noise(arg_keys[0], (K, LON, LAT), 1.0, 6.0, ((1, 32), (2, 4)), jnp.float32)
    land_mask = touch_ends((jax.random.randint(arg_keys[1], (LON, LAT), 0, 5) < 4).astype(jnp.int32), jax.random.fold_in(arg_keys[1], 1), 0, 1)
    pert_table = jnp.clip(jnp.exp(jax.random.uniform(arg_keys[2], (NPERT, K), jnp.float32, math.log(0.03), math.log(0.24))), 0.03, 0.24)
    pert_index = touch_ends(jax.random.randint(arg_keys[3], (MEMBERS,), 0, NPERT), jax.random.fold_in(arg_keys[3], 1), 0, NPERT - 1).astype(jnp.int32)
    base_kh = jnp.clip(jnp.exp(jax.random.uniform(arg_keys[4], (K,), jnp.float32, math.log(0.03), math.log(0.24))), 0.03, 0.24)
    member_mix = noise(arg_keys[5], (MEMBERS, K, K), (16 * K) ** -0.5, 0.15625, ((0, 4),))
    base_mix = noise(arg_keys[6], (K, K), (16 * K) ** -0.5, 0.15625)
    owner_keys = jax.random.split(jax.random.fold_in(arg_keys[7], 1), PROFILES // PROF_DEV)
    owner_turns = jax.random.permutation(jax.random.fold_in(arg_keys[7], 3), PROFILES // PROF_DEV)
    owner = jax.vmap(lambda own, number: deal_out(jax.random.fold_in(arg_keys[7], 2), own, number, PROF_DEV, N_LAT * N_LON, 1, CAP, 2))(owner_keys, owner_turns).reshape((PROFILES, 1))
    column = touch_ends(jax.random.randint(arg_keys[8], (PROFILES,), 0, CX * CY), jax.random.fold_in(arg_keys[8], 1), 0, (CX * CY) - 1).astype(jnp.int32)
    interp_w = jnp.clip(1.0 * jax.random.uniform(arg_keys[9], (PROFILES, K), jnp.float32) ** shard_levels(arg_keys[9], (PROFILES, K), ((0, 128),), -0.2, 0.2), 0.0, 1.0)
    obs_inv_var = jnp.clip(jnp.exp(math.log(16.0) - 2.7725887 * jax.random.uniform(arg_keys[10], (PROFILES, K), jnp.float32) ** shard_levels(arg_keys[10], (PROFILES, K), ((0, 128),), -0.2, 0.2)), 1.0, 16.0)
    observed = noise(arg_keys[11], (PROFILES, K), 1.0, 6.0, ((0, 128),), jnp.float32)
    return dict(initial_temp=initial_temp, land_mask=land_mask, pert_table=pert_table, pert_index=pert_index, base_kh=base_kh, member_mix=member_mix, base_mix=base_mix, owner=owner, column=column, interp_w=interp_w, obs_inv_var=obs_inv_var, observed=observed)


def advance_run(fields, kh_profile, mixing, ocean_open, has_next, has_prior):
    values = fields.astype(jnp.float32)
    laplace = jnp.roll(values, -1, 1) + jnp.roll(values, 1, 1) - 2.0 * values
    laplace = laplace + has_next * (jnp.roll(values, -1, 2) - values) + has_prior * (jnp.roll(values, 1, 2) - values)
    right_side = (values + kh_profile[:, None, None] * laplace).astype(jnp.bfloat16)
    right_float = right_side.astype(jnp.float32)
    vertical = right_float + jnp.einsum("kj,jab->kab", mixing.astype(jnp.float32), right_float, precision=lax.Precision.HIGHEST)
    return (values + ocean_open * (vertical - values)).astype(jnp.bfloat16)


def reference(initial_temp, land_mask, pert_table, pert_index, base_kh, member_mix, base_mix, owner, column, interp_w, obs_inv_var, observed):
    kh_runs = jnp.concatenate([pert_table[pert_index], base_kh[None, :]], 0)
    mix_runs = jnp.concatenate([member_mix, base_mix[None]], 0)
    ocean_open = land_mask.astype(jnp.float32)
    lat_rows = jnp.arange(LAT)
    has_next = (lat_rows < LAT - 1).astype(jnp.float32)
    has_prior = (lat_rows > 0).astype(jnp.float32)

    def run_one(pair):
        kh_profile, mixing = pair
        fields = initial_temp.astype(jnp.bfloat16)
        for step_index in range(STEPS):
            fields = advance_run(fields, kh_profile, mixing, ocean_open, has_next, has_prior)
        return fields

    finals = lax.map(run_one, (kh_runs, mix_runs))
    run_count = MEMBERS + 1
    target = owner[:, 0]
    lat_block = target // N_LON
    lon_block = target % N_LON
    global_lon = lon_block * CX + column // CY
    global_lat = lat_block * CY + column % CY
    column_flat = (global_lon * LAT + global_lat).astype(jnp.int32)
    picked = jnp.take(finals.reshape(run_count, K, LON * LAT), column_flat, axis=2).astype(jnp.float32)
    deeper = jnp.concatenate([picked[:, 1:], picked[:, -1:]], 1)
    weight = interp_w.T
    modeled = weight * picked + (1.0 - weight) * deeper
    green_cols = (modeled[:MEMBERS] - modeled[MEMBERS]).astype(jnp.bfloat16).astype(jnp.float32)
    misfit = observed.T - modeled[MEMBERS]
    normalizer = 1.0 / (PROFILES * K)
    weighted = green_cols * obs_inv_var.T
    gram_block = jnp.einsum("mkp,nkp->mn", weighted, green_cols, precision=lax.Precision.HIGHEST) * normalizer
    projection = jnp.einsum("mkp,kp->m", weighted, misfit, precision=lax.Precision.HIGHEST) * normalizer
    return finals[:MEMBERS], finals[MEMBERS], gram_block, projection, misfit.T
```

```python
import functools

import jax
import jax.numpy as jnp
from jax import lax
from jax.experimental import pallas as pl
from jax.experimental.pallas import tpu as pltpu
from jax.sharding import PartitionSpec as P

STEPS = 5
K = 100
KP = 128
CX = 4
CY = 128
CAP = 4
OWN = 128
REC = 256
HALO = 8
ROWS = CY + 2 * HALO
COLS = CX * CY
MEMBERS = 8
PAIRS = [(a, b) for a in range(MEMBERS) for b in range(a, MEMBERS)]
F32 = jnp.float32
BF16 = jnp.bfloat16
NT = (((1,), (1,)), ((), ()))
NN = (((1,), (0,)), ((), ()))
TN = (((0,), (0,)), ((), ()))
SMEM = pltpu.SMEM
VMEM = pltpu.VMEM


def dot(a, b, dims):
    return lax.dot_general(a, b, dims, preferred_element_type=F32)


def ones_where(cond):
    return jnp.where(cond, 1.0, 0.0).astype(BF16)


def iota(shape, dim):
    return lax.broadcasted_iota(jnp.int32, shape, dim)


def slots_kernel(m_ref, owner_ref, column_ref, w_ref, iv_ref, ob_ref, out_ref, code_ref, pad):
    owner = owner_ref[...]
    column = column_ref[...]
    hit = iota((OWN, REC), 0) == owner
    before = ones_where(iota((REC, REC), 0) < iota((REC, REC), 1))
    earlier = dot(ones_where(hit), before, NN)
    rank = jnp.sum(jnp.where(hit, earlier, 0.0), 0, keepdims=True).astype(jnp.int32)
    code_ref[...] = rank * OWN + owner
    slot = owner * CAP + rank
    mine = jnp.where(rank == m_ref[0], owner * CAP, -CAP)
    rows = iota((OWN * CAP, REC), 0)
    sub = iota((KP, REC), 0)
    high = (column // CY + 1).astype(F32)
    low = (column % CY).astype(F32)
    ids = jnp.where(sub == K, high, jnp.where(sub == K + 1, low, 0.0)).astype(BF16)
    placed = dot(ones_where(rows == slot), ids, NT)
    pad[...] = jnp.zeros((KP, REC), F32)
    for group, ref in enumerate((w_ref, iv_ref, ob_ref)):
        pad[0:K, :] = ref[...]
        placed += dot(ones_where(rows == mine + group), pad[...].astype(BF16), NT)
    out_ref[...] = placed.astype(BF16)


def window_kernel(
    m_ref, index_ref, own_ref, left_ref, right_ref, left2_ref, right2_ref, recv_ref,
    table_ref, base_kh_ref, mix_ref, base_mix_ref,
    fields_ref, picks_ref, base_ref,
    start, ping, pong, ocean, kh_pad, mix_pad, base_pad, slots,
):
    body = pl.ds(8, ROWS)

    def fill(column, cells):
        cells = cells.astype(F32)
        start[column, body, :] = cells
        ocean[column] = jnp.broadcast_to(cells[:, K : K + 1], (ROWS, KP))

    start[0, pl.ds(16, CY), :] = left2_ref[0].astype(F32)
    start[13, pl.ds(16, CY), :] = right2_ref[0].astype(F32)
    for first, ref in ((1, left_ref), (5, own_ref), (9, right_ref)):
        for c in range(CX):
            fill(first + c, ref[c])
    kh_pad[...] = jnp.zeros((8, KP), F32)
    kh_pad[0:1, 0:K] = table_ref[pl.ds(index_ref[0], 1), :]
    kh_pad[1:2, 0:K] = table_ref[pl.ds(index_ref[1], 1), :]
    kh_pad[2:3, 0:K] = base_kh_ref[...]
    mix_pad[...] = jnp.zeros((2 * KP, 2 * KP), BF16)
    mix_pad[0:K, 0:K] = mix_ref[0]
    mix_pad[KP : KP + K, KP : KP + K] = mix_ref[1]
    base_pad[...] = jnp.zeros((KP, KP), BF16)
    base_pad[0:K, 0:K] = base_mix_ref[...]

    for step in range(STEPS):
        source, target = ((ping, pong), (pong, ping))[step % 2]
        row0, count = (8, ROWS) if step < STEPS - 1 else (16, CY)

        def advance(column, _, step=step, source=source, target=target, row0=row0, count=count):
            def at(run, lon, row):
                if step == 0:
                    return start[lon, pl.ds(row, count), :]
                return source[run, lon, pl.ds(row, count), :]

            def around(run):
                return (at(run, column + 1, row0) + at(run, column - 1, row0)) + (
                    at(run, column, row0 + 1) + at(run, column, row0 - 1)
                )

            values, rights = [], []
            shared = (at(0, column, row0), around(0)) if step == 0 else None
            for run in range(3):
                value, near = shared if step == 0 else (at(run, column, row0), around(run))
                kh = kh_pad[run : run + 1, :]
                values.append(value)
                rights.append((value * (1.0 - 4.0 * kh) + near * kh).astype(BF16))
            both = dot(jnp.concatenate(rights[:2], 1), mix_pad[...], NT)
            mixed = (both[:, :KP], both[:, KP:], dot(rights[2], base_pad[...], NT))
            open_ = ocean[column, pl.ds(row0 - 8, count), :] > 0.0
            for run in range(3):
                vertical = rights[run].astype(F32) + mixed[run]
                new = jnp.where(open_, vertical, values[run])
                target[run, column, pl.ds(row0, count), :] = new.astype(BF16).astype(F32)
            return 0

        lax.fori_loop(step + 1, 13 - step, advance, 0)

    final = pong
    flat = []
    for run in range(3):
        parts = []
        for c in range(CX):
            cells = final[run, 5 + c, pl.ds(16, CY), :]
            fields_ref[run, c] = cells.T[0:K, :].astype(BF16)
            parts.append(cells.astype(BF16))
        flat.append(jnp.concatenate(parts, 0))
    both = jnp.concatenate(flat[:2], 1)

    slots[...] = recv_ref[...].astype(F32)
    cols = iota((OWN, COLS), 1)

    def chooser(ids):
        at = ((ids[:, K : K + 1] - 1.0) * CY + ids[:, K + 1 : K + 2]).astype(jnp.int32)
        return ones_where(at == cols)

    base_all = flat[2]
    own = jnp.zeros((OWN, KP), F32)
    for rank in range(CAP):
        pick = chooser(slots[pl.ds(rank, OWN, stride=CAP), :])
        picks_ref[rank] = dot(pick, both, NN).astype(BF16)
        own = jnp.where(m_ref[0] == rank, dot(pick, base_all, NN), own)
    base_ref[...] = own.astype(BF16)


def gram_kernel(m_ref, recv_ref, base_ref, slot_ref, out_ref, slots, greens, weighted, sums, rows2, *, scale):
    lane = iota((OWN, KP), 1)

    def deeper(x):
        return jnp.where(lane == K - 1, x, pltpu.roll(x, KP - 1, 1))

    slots[...] = slot_ref[...].astype(F32)
    weight = slots[pl.ds(0, OWN, stride=CAP), :]
    inv_var = jnp.where(lane < K, slots[pl.ds(1, OWN, stride=CAP), :], 0.0)
    measured = slots[pl.ds(2, OWN, stride=CAP), :]
    base = base_ref[...].astype(F32)

    def model(x):
        return weight * x + (1.0 - weight) * deeper(x)

    base_model = model(base)
    misfit = measured - base_model
    for member in range(MEMBERS):
        half = (member % 2) * KP
        picked = recv_ref[member // 2, :, half : half + KP].astype(F32)
        green = jnp.where(lane < K, model(picked) - base_model, 0.0).astype(BF16).astype(F32)
        greens[member] = green
        weighted[member] = green * inv_var
    sums[...] = jnp.zeros((KP, KP), F32)
    for i, (a, b) in enumerate(PAIRS):
        sums[i : i + 1, :] = jnp.sum(weighted[a] * greens[b], 0, keepdims=True)
    for a in range(MEMBERS):
        sums[len(PAIRS) + a : len(PAIRS) + a + 1, :] = jnp.sum(weighted[a] * misfit, 0, keepdims=True)
    total = jnp.sum(sums[...].T, 0, keepdims=True) * scale
    high = total.astype(BF16).astype(F32)
    rest = total - high
    line = iota((1, KP), 1)
    both = jnp.where(line < 64, high, pltpu.roll(jnp.broadcast_to(rest, (8, KP)), 64, 1)[0:1])
    rows2[pl.ds(0, OWN, stride=2), :] = base
    rows2[pl.ds(1, OWN, stride=2), :] = jnp.broadcast_to(both, (OWN, KP))
    packed = rows2[...].astype(BF16)
    for copy in range(4):
        out_ref[copy] = packed


def result_kernel(recv_ref, code_ref, w_ref, ob_ref, misfit_ref, gram_ref, proj_ref):
    recv = recv_ref[...]
    count = recv.shape[0]
    pick = ones_where(iota((count, REC), 0) == 2 * code_ref[...])
    picked = dot(recv, pick, TN)
    values = picked[0:K]
    deeper = jnp.concatenate([picked[1:K], picked[K - 1 : K]], 0)
    weight = w_ref[...]
    misfit_ref[...] = ob_ref[...] - (weight * values + (1.0 - weight) * deeper)
    odd = iota((8, KP), 0) % 2 == 1
    part = jnp.sum(recv.astype(F32).reshape(count // 8, 8, KP), 0)
    total = jnp.sum(jnp.where(odd, part, 0.0), 0, keepdims=True)
    total = jnp.broadcast_to(total, (8, KP))
    total = total + pltpu.roll(total, 64, 1)
    sub, line = iota((8, KP), 0), iota((8, KP), 1)
    gram = jnp.zeros((8, KP), F32)
    for i, (a, b) in enumerate(PAIRS):
        here = ((sub == a) & (line == b)) | ((sub == b) & (line == a))
        gram = jnp.where(here, total[:, i : i + 1], gram)
    gram_ref[...] = gram[:, 0:MEMBERS]
    proj_ref[...] = pltpu.roll(total, KP - len(PAIRS), 1)[0:1, 0:MEMBERS]


def vmem(count):
    return [pl.BlockSpec(memory_space=VMEM)] * count


def smem(count):
    return [pl.BlockSpec(memory_space=SMEM)] * count


def on_device(
    initial_temp, land_mask, pert_table, pert_index, base_kh, member_mix, base_mix,
    owner, column, interp_w, obs_inv_var, observed,
):
    owners = ("lat", "lon")
    mem = lax.axis_index("mem").astype(jnp.int32).reshape(1)
    lat_at, lat_count = lax.axis_index("lat"), lax.axis_size("lat")
    lon_count = lax.axis_size("lon")
    w_t, iv_t, ob_t = interp_w.T, obs_inv_var.T, observed.T

    send, code = pl.pallas_call(
        slots_kernel,
        out_shape=(
            jax.ShapeDtypeStruct((OWN * CAP, KP), BF16),
            jax.ShapeDtypeStruct((1, REC), jnp.int32),
        ),
        in_specs=smem(1) + vmem(5),
        out_specs=tuple(vmem(2)),
        scratch_shapes=[VMEM((KP, REC), F32)],
        name="slots",
    )(mem, owner.reshape(1, REC), column.reshape(1, REC), w_t, iv_t, ob_t)

    cells = jnp.transpose(initial_temp, (1, 2, 0)).astype(BF16)
    cells = jnp.concatenate(
        [
            cells,
            land_mask.astype(BF16)[:, :, None],
            jnp.zeros((CX, CY, KP - K - 1), BF16),
        ],
        2,
    )
    up = [(i, i + 1) for i in range(lat_count - 1)]
    down = [(i + 1, i) for i in range(lat_count - 1)]
    below = lax.ppermute(cells[:, CY - HALO :], "lat", up)
    above = lax.ppermute(cells[:, :HALO], "lat", down)
    below = jnp.where(lat_at == 0, cells[:, :HALO][:, ::-1], below)
    above = jnp.where(lat_at == lat_count - 1, cells[:, CY - HALO :][:, ::-1], above)
    tall = jnp.concatenate([below, cells, above], 1)

    def shift(x, by):
        return lax.ppermute(x, "lon", [(i, (i + by) % lon_count) for i in range(lon_count)])

    left2, right2 = shift(cells[CX - 1 :], 2), shift(cells[:1], -2)
    left, right = shift(tall, 1), shift(tall, -1)
    recv = lax.all_to_all(
        send.reshape(OWN, CAP, KP), owners, split_axis=0, concat_axis=0, tiled=True
    ).reshape(OWN * CAP, KP)

    fields, picks, base_rows = pl.pallas_call(
        window_kernel,
        out_shape=(
            jax.ShapeDtypeStruct((3, CX, K, CY), BF16),
            jax.ShapeDtypeStruct((CAP, OWN, 2 * KP), BF16),
            jax.ShapeDtypeStruct((OWN, KP), BF16),
        ),
        in_specs=smem(2) + vmem(10),
        out_specs=tuple(vmem(3)),
        scratch_shapes=[
            VMEM((14, ROWS + 16, KP), F32),
            VMEM((3, 14, ROWS + 16, KP), F32),
            VMEM((3, 14, ROWS + 16, KP), F32),
            VMEM((14, ROWS, KP), F32),
            VMEM((8, KP), F32),
            VMEM((2 * KP, 2 * KP), BF16),
            VMEM((KP, KP), BF16),
            VMEM((OWN * CAP, KP), F32),
        ],
        name="window",
    )(
        mem, pert_index, tall, left, right, left2, right2, recv,
        pert_table, base_kh.reshape(1, K), member_mix, base_mix,
    )

    members = lax.all_to_all(picks, "mem", split_axis=0, concat_axis=0, tiled=True)
    back = pl.pallas_call(
        functools.partial(gram_kernel, scale=1.0 / (OWN * REC * K)),
        out_shape=jax.ShapeDtypeStruct((4, 2 * OWN, KP), BF16),
        in_specs=smem(1) + vmem(3),
        out_specs=vmem(1)[0],
        scratch_shapes=[
            VMEM((OWN * CAP, KP), F32),
            VMEM((MEMBERS, OWN, KP), F32),
            VMEM((MEMBERS, OWN, KP), F32),
            VMEM((KP, KP), F32),
            VMEM((2 * OWN, KP), F32),
        ],
        name="gram",
    )(mem, members, base_rows, recv)

    returned = lax.all_to_all(
        back.reshape(4 * OWN, 2, KP), ("mem", "lat", "lon"), split_axis=0, concat_axis=0, tiled=True
    ).reshape(8 * OWN, KP)
    misfit_t, gram, proj = pl.pallas_call(
        result_kernel,
        out_shape=(
            jax.ShapeDtypeStruct((K, REC), F32),
            jax.ShapeDtypeStruct((MEMBERS, MEMBERS), F32),
            jax.ShapeDtypeStruct((1, MEMBERS), F32),
        ),
        in_specs=vmem(4),
        out_specs=tuple(vmem(3)),
        name="result",
    )(returned, code, w_t, ob_t)

    fields = jnp.transpose(fields, (0, 2, 1, 3))
    return fields[:2], fields[2], gram, proj.reshape(MEMBERS), misfit_t.T


def solution(mesh):
    placed = (
        P(None, "lon", "lat"),
        P("lon", "lat"),
        P(),
        P("mem"),
        P(),
        P("mem", None, None),
        P(),
        P(("lat", "lon"), None),
        P(("lat", "lon")),
        P(("lat", "lon"), None),
        P(("lat", "lon"), None),
        P(("lat", "lon"), None),
    )
    return jax.shard_map(
        on_device,
        mesh=mesh,
        in_specs=placed,
        out_specs=(
            P("mem", None, "lon", "lat"),
            P(None, "lon", "lat"),
            P(),
            P(),
            P(("lat", "lon"), None),
        ),
        check_vma=False,
    )
```

```python
import functools

import jax
import jax.numpy as jnp
from jax import lax
from jax.experimental import pallas as pl
from jax.experimental.pallas import tpu as pltpu
from jax.sharding import PartitionSpec as P


STEPS = 5
BLOCK = (4, 5, 4, 6, 4)
K = 100
KP = 128
SPARE = KP - K
CX = 4
CY = 128
CAP = 4
OWN = 128
REC = 256
HALO = 8
ROWS = CY + 2 * HALO
COLS = CX * CY
MEMBERS = 8
PAIRS = [(a, b) for a in range(MEMBERS) for b in range(a, MEMBERS)]
F32 = jnp.float32
BF16 = jnp.bfloat16
NT = (((1,), (1,)), ((), ()))
NN = (((1,), (0,)), ((), ()))
TN = (((0,), (0,)), ((), ()))
SMEM = pltpu.SMEM
VMEM = pltpu.VMEM


def dot(a, b, dims):
    return lax.dot_general(a, b, dims, preferred_element_type=F32)


def ones_where(cond):
    return jnp.where(cond, 1.0, 0.0).astype(BF16)


def iota(shape, dim):
    return lax.broadcasted_iota(jnp.int32, shape, dim)


def slots_kernel(m_ref, owner_ref, column_ref, w_ref, iv_ref, ob_ref, out_ref, code_ref, pad):
    owner = owner_ref[...]
    column = column_ref[...]
    hit = iota((OWN, REC), 0) == owner
    before = ones_where(iota((REC, REC), 0) < iota((REC, REC), 1))
    earlier = dot(ones_where(hit), before, NN)
    rank = jnp.sum(jnp.where(hit, earlier, 0.0), 0, keepdims=True).astype(jnp.int32)
    slot = owner * CAP + rank
    code_ref[...] = slot
    mine = jnp.where(rank == m_ref[0], owner * CAP, -CAP)
    rows = iota((OWN * CAP, REC), 0)
    sub = iota((KP, REC), 0)
    high = (column // CY + 1).astype(F32)
    low = (column % CY).astype(F32)
    ids = jnp.where(sub == K, high, jnp.where(sub == K + 1, low, 0.0)).astype(BF16)
    placed = dot(ones_where(rows == slot), ids, NT)
    pad[...] = jnp.zeros((KP, REC), F32)
    for group, ref in enumerate((w_ref, iv_ref, ob_ref)):
        pad[0:K, :] = ref[...]
        placed += dot(ones_where(rows == mine + group), pad[...].astype(BF16), NT)
    out_ref[...] = placed.astype(BF16)


def window_kernel(
    index_ref, own_ref, left_ref, right_ref, left2_ref, right2_ref, recv_ref,
    table_ref, base_kh_ref, mix_ref, base_mix_ref,
    fields_ref, picks_ref, base_ref,
    start, ping, pong, ocean, kh_pad, mix_pad, one_pad, base_pad, first, second,
):
    body = pl.ds(8, ROWS)

    def fill(column, cells):
        cells = cells.astype(F32)
        start[column, body, :] = cells
        ocean[column] = jnp.broadcast_to(cells[:, K : K + 1], (ROWS, KP))

    start[0, pl.ds(16, CY), :] = left2_ref[0].astype(F32)
    start[13, pl.ds(16, CY), :] = right2_ref[0].astype(F32)
    for place, ref in ((1, left_ref), (5, own_ref), (9, right_ref)):
        for c in range(CX):
            fill(place + c, ref[c])
    kh_pad[...] = jnp.zeros((8, KP), F32)
    kh_pad[0:1, 0:K] = table_ref[pl.ds(index_ref[0], 1), :]
    kh_pad[1:2, 0:K] = table_ref[pl.ds(index_ref[1], 1), :]
    kh_pad[2:3, 0:K] = base_kh_ref[...]
    mix_pad[...] = jnp.zeros((2 * KP, 2 * KP), BF16)
    mix_pad[0:K, 0:K] = mix_ref[0]
    mix_pad[KP : KP + K, KP : KP + K] = mix_ref[1]
    same = iota((KP, KP), 0) == iota((KP, KP), 1)
    one_pad[...] = jnp.zeros((2 * KP, 2 * KP), BF16)
    one_pad[0:KP, 0:KP] = ones_where(same)
    one_pad[KP:, KP:] = ones_where(same)
    base_pad[...] = jnp.zeros((KP, 2 * KP), BF16)
    base_pad[0:K, 0:K] = base_mix_ref[...]
    base_pad[:, KP:] = ones_where(same)

    for step in range(STEPS):
        source, target = ((ping, pong), (pong, ping))[step % 2]
        row0, count = (8, ROWS) if step < STEPS - 1 else (16, CY)

        def advance(column, step=step, source=source, target=target, row0=row0, count=count):
            def at(run, lon, row):
                if step == 0:
                    return start[lon, pl.ds(row, count), :]
                return source[run, lon, pl.ds(row, count), :]

            def around(run):
                return (at(run, column + 1, row0) + at(run, column - 1, row0)) + (
                    at(run, column, row0 + 1) + at(run, column, row0 - 1)
                )

            values, rights = [], []
            shared = (at(0, column, row0), around(0)) if step == 0 else None
            for run in range(3):
                value, near = shared if step == 0 else (at(run, column, row0), around(run))
                kh = kh_pad[run : run + 1, :]
                values.append(value)
                rights.append((value * (1.0 - 4.0 * kh) + near * kh).astype(BF16))
            pair = jnp.concatenate(rights[:2], 1)
            both = dot(pair, mix_pad[...], NT) + dot(pair, one_pad[...], NT)
            twice = jnp.concatenate([rights[2], rights[2]], 1)
            mixed = (both[:, :KP], both[:, KP:], dot(twice, base_pad[...], NT))
            open_ = ocean[column, pl.ds(row0 - 8, count), :] > 0.0
            for run in range(3):
                new = jnp.where(open_, mixed[run], values[run])
                target[run, column, pl.ds(row0, count), :] = new.astype(BF16).astype(F32)

        columns = 12 - 2 * step
        block = BLOCK[step]

        def several(turn, _, step=step, block=block, advance=advance):
            for c in range(block):
                advance(step + 1 + turn * block + c)
            return 0

        if columns == block:
            several(0, 0)
        else:
            lax.fori_loop(0, columns // block, several, 0)

    final = pong
    flat = []
    for run in range(3):
        parts = []
        for c in range(CX):
            cells = final[run, 5 + c, pl.ds(16, CY), :]
            fields_ref[run, c] = cells.T[0:K, :].astype(BF16)
            parts.append(cells.astype(BF16))
        flat.append(jnp.concatenate(parts, 0))
    ids = recv_ref[...].astype(F32)
    at = ((ids[:, K : K + 1] - 1.0) * CY + ids[:, K + 1 : K + 2]).astype(jnp.int32)
    pick = ones_where(at == iota((OWN * CAP, COLS), 1))
    base_ref[...] = dot(pick, flat[2], NN).astype(BF16)
    both = dot(pick, jnp.concatenate(flat[:2], 1), NN)
    for half, scratch in enumerate((first, second)):
        scratch[...] = both[:, half * KP : (half + 1) * KP]
        for rank in range(CAP):
            picked = scratch[pl.ds(rank, OWN, stride=CAP), :]
            picks_ref[rank, :, half * KP : (half + 1) * KP] = picked.astype(BF16)


def gram_kernel(m_ref, recv_ref, base_ref, slot_ref, out_ref, slots, bases, greens, weighted, sums, *, scale):
    lane = iota((OWN, KP), 1)

    def deeper(x):
        return jnp.where(lane == K - 1, x, pltpu.roll(x, KP - 1, 1))

    slots[...] = slot_ref[...].astype(F32)
    weight = slots[pl.ds(0, OWN, stride=CAP), :]
    inv_var = jnp.where(lane < K, slots[pl.ds(1, OWN, stride=CAP), :], 0.0)
    measured = slots[pl.ds(2, OWN, stride=CAP), :]
    bases[...] = base_ref[...].astype(F32)
    base = bases[pl.ds(0, OWN, stride=CAP), :]
    for rank in range(1, CAP):
        base = jnp.where(m_ref[0] == rank, bases[pl.ds(rank, OWN, stride=CAP), :], base)

    def model(x):
        return weight * x + (1.0 - weight) * deeper(x)

    base_model = model(base)
    misfit = measured - base_model
    for member in range(MEMBERS):
        half = (member % 2) * KP
        picked = recv_ref[member // 2, :, half : half + KP].astype(F32)
        green = jnp.where(lane < K, model(picked) - base_model, 0.0).astype(BF16).astype(F32)
        greens[member] = green
        weighted[member] = green * inv_var
    sums[...] = jnp.zeros((KP, KP), F32)
    for i, (a, b) in enumerate(PAIRS):
        sums[i : i + 1, :] = jnp.sum(weighted[a] * greens[b], 0, keepdims=True)
    for a in range(MEMBERS):
        sums[len(PAIRS) + a : len(PAIRS) + a + 1, :] = jnp.sum(weighted[a] * misfit, 0, keepdims=True)
    total = jnp.sum(sums[...].T, 0, keepdims=True) * scale
    high = total.astype(BF16).astype(F32)
    high = jnp.broadcast_to(high, (8, KP))
    rest = jnp.broadcast_to(total, (8, KP)) - high
    turn = iota((8, KP), 0) % CAP
    tail = jnp.where(
        turn == 0,
        pltpu.roll(high, K, 1),
        jnp.where(
            turn == 1,
            pltpu.roll(high, K - SPARE, 1),
            jnp.where(turn == 2, pltpu.roll(rest, K, 1), pltpu.roll(rest, K - SPARE, 1)),
        ),
    )
    rows = bases[...].reshape(OWN * CAP // 8, 8, KP)
    rows = jnp.where(iota((1, 8, KP), 2) < K, rows, tail[None])
    out_ref[...] = rows.reshape(OWN * CAP, KP).astype(BF16)


def result_kernel(recv_ref, code_ref, w_ref, ob_ref, misfit_ref, gram_ref, proj_ref):
    recv = recv_ref[...]
    pick = ones_where(iota((OWN * CAP, REC), 0) == code_ref[...])
    picked = dot(recv, pick, TN)
    values = picked[0:K]
    deeper = jnp.concatenate([picked[1:K], picked[K - 1 : K]], 0)
    weight = w_ref[...]
    misfit_ref[...] = ob_ref[...] - (weight * values + (1.0 - weight) * deeper)
    part = jnp.sum(recv.astype(F32).reshape(OWN * CAP // 8, 8, KP), 0)
    part = part + pltpu.roll(part, 4, 0)
    part = part + pltpu.roll(part, 6, 0)
    sub, line = iota((8, KP), 0), iota((8, KP), 1)
    total = jnp.where(
        line < SPARE,
        pltpu.roll(jnp.broadcast_to(part[0:1], (8, KP)), SPARE, 1),
        pltpu.roll(jnp.broadcast_to(part[1:2], (8, KP)), 2 * SPARE, 1),
    )
    gram = jnp.zeros((8, KP), F32)
    for i, (a, b) in enumerate(PAIRS):
        here = ((sub == a) & (line == b)) | ((sub == b) & (line == a))
        gram = jnp.where(here, total[:, i : i + 1], gram)
    gram_ref[...] = gram[:, 0:MEMBERS]
    proj_ref[...] = pltpu.roll(total, KP - len(PAIRS), 1)[0:1, 0:MEMBERS]


def near(x):
    return pltpu.with_memory_space_constraint(x, VMEM)


def vmem(count):
    return [pl.BlockSpec(memory_space=VMEM)] * count


def smem(count):
    return [pl.BlockSpec(memory_space=SMEM)] * count


def on_device(
    initial_temp, land_mask, pert_table, pert_index, base_kh, member_mix, base_mix,
    owner, column, interp_w, obs_inv_var, observed,
):
    owners = ("lat", "lon")
    mem = lax.axis_index("mem").astype(jnp.int32).reshape(1)
    lat_at, lat_count = lax.axis_index("lat"), lax.axis_size("lat")
    lon_count = lax.axis_size("lon")
    w_t, iv_t, ob_t = interp_w.T, obs_inv_var.T, observed.T

    cells = jnp.transpose(initial_temp, (1, 2, 0)).astype(BF16)
    cells = jnp.concatenate(
        [
            cells,
            land_mask.astype(BF16)[:, :, None],
            jnp.zeros((CX, CY, KP - K - 1), BF16),
        ],
        2,
    )
    up = [(i, i + 1) for i in range(lat_count - 1)]
    down = [(i + 1, i) for i in range(lat_count - 1)]
    below = lax.ppermute(cells[:, CY - HALO :], "lat", up)
    above = lax.ppermute(cells[:, :HALO], "lat", down)
    below = jnp.where(lat_at == 0, cells[:, :HALO][:, ::-1], below)
    above = jnp.where(lat_at == lat_count - 1, cells[:, CY - HALO :][:, ::-1], above)
    tall = jnp.concatenate([below, cells, above], 1)

    def shift(x, by):
        return lax.ppermute(x, "lon", [(i, (i + by) % lon_count) for i in range(lon_count)])

    left2 = shift(cells[CX - 1 :], 2)
    right2 = shift(cells[:1], -2)
    left = shift(tall, 1)
    right = shift(tall, -1)

    owner_row, column_row, tall = lax.optimization_barrier(
        (owner.reshape(1, REC), column.reshape(1, REC), tall)
    )
    send, code = pl.pallas_call(
        slots_kernel,
        out_shape=(VMEM((OWN * CAP, KP), BF16), VMEM((1, REC), jnp.int32)),
        in_specs=smem(1) + vmem(5),
        out_specs=tuple(vmem(2)),
        scratch_shapes=[VMEM((KP, REC), F32)],
        name="slots",
    )(mem, owner_row, column_row, w_t, iv_t, ob_t)
    recv = lax.all_to_all(
        send.reshape(OWN, CAP, KP), owners, split_axis=0, concat_axis=0, tiled=True
    )
    recv = recv.reshape(OWN * CAP, KP)

    fields, picks, base_rows = pl.pallas_call(
        window_kernel,
        out_shape=(
            VMEM((3, CX, K, CY), BF16),
            VMEM((CAP, OWN, 2 * KP), BF16),
            VMEM((OWN * CAP, KP), BF16),
        ),
        in_specs=smem(1) + vmem(10),
        out_specs=tuple(vmem(3)),
        scratch_shapes=[
            VMEM((14, ROWS + 16, KP), F32),
            VMEM((3, 14, ROWS + 16, KP), F32),
            VMEM((3, 14, ROWS + 16, KP), F32),
            VMEM((14, ROWS, KP), F32),
            VMEM((8, KP), F32),
            VMEM((2 * KP, 2 * KP), BF16),
            VMEM((2 * KP, 2 * KP), BF16),
            VMEM((KP, 2 * KP), BF16),
            VMEM((OWN * CAP, KP), F32),
            VMEM((OWN * CAP, KP), F32),
        ],
        name="window",
    )(
        pert_index, near(tall), near(left), near(right), near(left2), near(right2), near(recv),
        pert_table, base_kh.reshape(1, K), member_mix, base_mix,
    )

    members = lax.all_to_all(picks, "mem", split_axis=0, concat_axis=0, tiled=True)
    back = pl.pallas_call(
        functools.partial(gram_kernel, scale=1.0 / (OWN * REC * K)),
        out_shape=VMEM((OWN * CAP, KP), BF16),
        in_specs=smem(1) + vmem(3),
        out_specs=vmem(1)[0],
        scratch_shapes=[
            VMEM((OWN * CAP, KP), F32),
            VMEM((OWN * CAP, KP), F32),
            VMEM((MEMBERS, OWN, KP), F32),
            VMEM((MEMBERS, OWN, KP), F32),
            VMEM((KP, KP), F32),
        ],
        name="gram",
    )(mem, near(members), near(base_rows), near(recv))

    returned = lax.all_to_all(
        back.reshape(OWN, CAP, KP), owners, split_axis=0, concat_axis=0, tiled=True
    ).reshape(OWN * CAP, KP)
    misfit_t, gram, proj = pl.pallas_call(
        result_kernel,
        out_shape=(
            jax.ShapeDtypeStruct((K, REC), F32),
            jax.ShapeDtypeStruct((MEMBERS, MEMBERS), F32),
            jax.ShapeDtypeStruct((1, MEMBERS), F32),
        ),
        in_specs=vmem(4),
        out_specs=tuple(vmem(3)),
        name="result",
    )(near(returned), near(code), w_t, ob_t)
    gram, proj = lax.psum((gram, proj), "mem")

    fields = jnp.transpose(fields, (0, 2, 1, 3))
    return fields[:2], fields[2], gram, proj.reshape(MEMBERS), misfit_t.T


def solution(mesh):
    placed = (
        P(None, "lon", "lat"),
        P("lon", "lat"),
        P(),
        P("mem"),
        P(),
        P("mem", None, None),
        P(),
        P(("lat", "lon"), None),
        P(("lat", "lon")),
        P(("lat", "lon"), None),
        P(("lat", "lon"), None),
        P(("lat", "lon"), None),
    )
    return jax.shard_map(
        on_device,
        mesh=mesh,
        in_specs=placed,
        out_specs=(
            P("mem", None, "lon", "lat"),
            P(None, "lon", "lat"),
            P(),
            P(),
            P(("lat", "lon"), None),
        ),
        check_vma=False,
    )
```

```python
import functools

import jax
import jax.numpy as jnp
from jax import lax
from jax.experimental import pallas as pl
from jax.experimental.pallas import tpu as pltpu
from jax.sharding import PartitionSpec as P


STEPS = 5
BLOCK = (4, 5, 4, 6, 4)
K = 100
KP = 128
SPARE = KP - K
CX = 4
CY = 128
CAP = 4
OWN = 128
REC = 256
HALO = 8
ROWS = CY + 2 * HALO
COLS = CX * CY
MEMBERS = 8
PAIRS = [(a, b) for a in range(MEMBERS) for b in range(a, MEMBERS)]
F32 = jnp.float32
BF16 = jnp.bfloat16
NT = (((1,), (1,)), ((), ()))
NN = (((1,), (0,)), ((), ()))
TN = (((0,), (0,)), ((), ()))
SMEM = pltpu.SMEM
VMEM = pltpu.VMEM


def dot(a, b, dims):
    return lax.dot_general(a, b, dims, preferred_element_type=F32)


def ones_where(cond):
    return jnp.where(cond, 1.0, 0.0).astype(BF16)


def iota(shape, dim):
    return lax.broadcasted_iota(jnp.int32, shape, dim)


def slots_kernel(m_ref, owner_ref, column_ref, w_ref, iv_ref, ob_ref, out_ref, code_ref, pad):
    owner = owner_ref[...]
    column = column_ref[...]
    hit = iota((OWN, REC), 0) == owner
    before = ones_where(iota((REC, REC), 0) < iota((REC, REC), 1))
    earlier = dot(ones_where(hit), before, NN)
    rank = jnp.sum(jnp.where(hit, earlier, 0.0), 0, keepdims=True).astype(jnp.int32)
    slot = owner * CAP + rank
    code_ref[...] = slot
    mine = jnp.where(rank == m_ref[0], owner * CAP, -CAP)
    rows = iota((OWN * CAP, REC), 0)
    sub = iota((KP, REC), 0)
    high = (column // CY + 1).astype(F32)
    low = (column % CY).astype(F32)
    ids = jnp.where(sub == K, high, jnp.where(sub == K + 1, low, 0.0)).astype(BF16)
    placed = dot(ones_where(rows == slot), ids, NT)
    pad[...] = jnp.zeros((KP, REC), F32)
    for group, ref in enumerate((w_ref, iv_ref, ob_ref)):
        pad[0:K, :] = ref[...]
        placed += dot(ones_where(rows == mine + group), pad[...].astype(BF16), NT)
    out_ref[...] = placed.astype(BF16)


def window_kernel(
    index_ref, own_ref, left_ref, right_ref, left2_ref, right2_ref, recv_ref,
    table_ref, base_kh_ref, mix_ref, base_mix_ref,
    fields_ref, picks_ref, base_ref,
    start, ping, pong, ocean, kh_pad, mix_pad, one_pad, base_pad, first, second,
):
    body = pl.ds(8, ROWS)

    def fill(column, cells):
        cells = cells.astype(F32)
        start[column, body, :] = cells
        ocean[column] = jnp.broadcast_to(cells[:, K : K + 1], (ROWS, KP))

    start[0, pl.ds(16, CY), :] = left2_ref[0].astype(F32)
    start[13, pl.ds(16, CY), :] = right2_ref[0].astype(F32)
    for place, ref in ((1, left_ref), (5, own_ref), (9, right_ref)):
        for c in range(CX):
            fill(place + c, ref[c])
    kh_pad[...] = jnp.zeros((8, KP), F32)
    kh_pad[0:1, 0:K] = table_ref[pl.ds(index_ref[0], 1), :]
    kh_pad[1:2, 0:K] = table_ref[pl.ds(index_ref[1], 1), :]
    kh_pad[2:3, 0:K] = base_kh_ref[...]
    mix_pad[...] = jnp.zeros((2 * KP, 2 * KP), BF16)
    mix_pad[0:K, 0:K] = mix_ref[0]
    mix_pad[KP : KP + K, KP : KP + K] = mix_ref[1]
    same = iota((KP, KP), 0) == iota((KP, KP), 1)
    one_pad[...] = jnp.zeros((2 * KP, 2 * KP), BF16)
    one_pad[0:KP, 0:KP] = ones_where(same)
    one_pad[KP:, KP:] = ones_where(same)
    base_pad[...] = jnp.zeros((KP, 2 * KP), BF16)
    base_pad[0:K, 0:K] = base_mix_ref[...]
    base_pad[:, KP:] = ones_where(same)

    for step in range(STEPS):
        source, target = ((ping, pong), (pong, ping))[step % 2]
        row0, count = (8, ROWS) if step < STEPS - 1 else (16, CY)

        def advance(column, step=step, source=source, target=target, row0=row0, count=count):
            def at(run, lon, row):
                if step == 0:
                    return start[lon, pl.ds(row, count), :]
                return source[run, lon, pl.ds(row, count), :]

            def around(run):
                return (at(run, column + 1, row0) + at(run, column - 1, row0)) + (
                    at(run, column, row0 + 1) + at(run, column, row0 - 1)
                )

            values, rights = [], []
            shared = (at(0, column, row0), around(0)) if step == 0 else None
            for run in range(3):
                value, near = shared if step == 0 else (at(run, column, row0), around(run))
                kh = kh_pad[run : run + 1, :]
                values.append(value)
                rights.append((value * (1.0 - 4.0 * kh) + near * kh).astype(BF16))
            pair = jnp.concatenate(rights[:2], 1)
            both = dot(pair, mix_pad[...], NT) + dot(pair, one_pad[...], NT)
            twice = jnp.concatenate([rights[2], rights[2]], 1)
            mixed = (both[:, :KP], both[:, KP:], dot(twice, base_pad[...], NT))
            open_ = ocean[column, pl.ds(row0 - 8, count), :] > 0.0
            for run in range(3):
                new = jnp.where(open_, mixed[run], values[run])
                target[run, column, pl.ds(row0, count), :] = new.astype(BF16).astype(F32)

        columns = 12 - 2 * step
        block = BLOCK[step]

        def several(turn, _, step=step, block=block, advance=advance):
            for c in range(block):
                advance(step + 1 + turn * block + c)
            return 0

        if columns == block:
            several(0, 0)
        else:
            lax.fori_loop(0, columns // block, several, 0)

    final = pong
    flat = []
    for run in range(3):
        parts = []
        for c in range(CX):
            cells = final[run, 5 + c, pl.ds(16, CY), :]
            fields_ref[run, c] = cells.T[0:K, :].astype(BF16)
            parts.append(cells.astype(BF16))
        flat.append(jnp.concatenate(parts, 0))
    ids = recv_ref[...].astype(F32)
    at = ((ids[:, K : K + 1] - 1.0) * CY + ids[:, K + 1 : K + 2]).astype(jnp.int32)
    pick = ones_where(at == iota((OWN * CAP, COLS), 1))
    base_ref[...] = dot(pick, flat[2], NN).astype(BF16)
    both = dot(pick, jnp.concatenate(flat[:2], 1), NN)
    for half, scratch in enumerate((first, second)):
        scratch[...] = both[:, half * KP : (half + 1) * KP]
        for rank in range(CAP):
            picked = scratch[pl.ds(rank, OWN, stride=CAP), :]
            picks_ref[rank, :, half * KP : (half + 1) * KP] = picked.astype(BF16)


def gram_kernel(m_ref, recv_ref, base_ref, slot_ref, out_ref, slots, bases, greens, weighted, sums, *, scale):
    lane = iota((OWN, KP), 1)

    def deeper(x):
        return jnp.where(lane == K - 1, x, pltpu.roll(x, KP - 1, 1))

    slots[...] = slot_ref[...].astype(F32)
    weight = slots[pl.ds(0, OWN, stride=CAP), :]
    inv_var = jnp.where(lane < K, slots[pl.ds(1, OWN, stride=CAP), :], 0.0)
    measured = slots[pl.ds(2, OWN, stride=CAP), :]
    bases[...] = base_ref[...].astype(F32)
    base = bases[pl.ds(0, OWN, stride=CAP), :]
    for rank in range(1, CAP):
        base = jnp.where(m_ref[0] == rank, bases[pl.ds(rank, OWN, stride=CAP), :], base)

    def model(x):
        return weight * x + (1.0 - weight) * deeper(x)

    base_model = model(base)
    misfit = measured - base_model
    for member in range(MEMBERS):
        half = (member % 2) * KP
        picked = recv_ref[member // 2, :, half : half + KP].astype(F32)
        green = jnp.where(lane < K, model(picked) - base_model, 0.0).astype(BF16).astype(F32)
        greens[member] = green
        weighted[member] = green * inv_var
    sums[...] = jnp.zeros((KP, KP), F32)
    for i, (a, b) in enumerate(PAIRS):
        sums[i : i + 1, :] = jnp.sum(weighted[a] * greens[b], 0, keepdims=True)
    for a in range(MEMBERS):
        sums[len(PAIRS) + a : len(PAIRS) + a + 1, :] = jnp.sum(weighted[a] * misfit, 0, keepdims=True)
    total = jnp.sum(sums[...].T, 0, keepdims=True) * scale
    high = total.astype(BF16).astype(F32)
    high = jnp.broadcast_to(high, (8, KP))
    rest = jnp.broadcast_to(total, (8, KP)) - high
    turn = iota((8, KP), 0) % CAP
    tail = jnp.where(
        turn == 0,
        pltpu.roll(high, K, 1),
        jnp.where(
            turn == 1,
            pltpu.roll(high, K - SPARE, 1),
            jnp.where(turn == 2, pltpu.roll(rest, K, 1), pltpu.roll(rest, K - SPARE, 1)),
        ),
    )
    rows = bases[...].reshape(OWN * CAP // 8, 8, KP)
    rows = jnp.where(iota((1, 8, KP), 2) < K, rows, tail[None])
    out_ref[...] = rows.reshape(OWN * CAP, KP).astype(BF16)


def result_kernel(recv_ref, code_ref, w_ref, ob_ref, misfit_ref, sums_ref):
    recv = recv_ref[...]
    pick = ones_where(iota((OWN * CAP, REC), 0) == code_ref[...])
    picked = dot(recv, pick, TN)
    values = picked[0:K]
    deeper = jnp.concatenate([picked[1:K], picked[K - 1 : K]], 0)
    weight = w_ref[...]
    misfit_ref[...] = ob_ref[...] - (weight * values + (1.0 - weight) * deeper)
    part = jnp.sum(recv.astype(F32).reshape(OWN * CAP // 8, 8, KP), 0)
    part = part + pltpu.roll(part, 4, 0)
    part = part + pltpu.roll(part, 6, 0)
    sub, line = iota((8, KP), 0), iota((8, KP), 1)
    total = jnp.where(
        line < SPARE,
        pltpu.roll(jnp.broadcast_to(part[0:1], (8, KP)), SPARE, 1),
        pltpu.roll(jnp.broadcast_to(part[1:2], (8, KP)), 2 * SPARE, 1),
    )
    gram = jnp.zeros((8, KP), F32)
    for i, (a, b) in enumerate(PAIRS):
        here = ((sub == a) & (line == b)) | ((sub == b) & (line == a))
        gram = jnp.where(here, total[:, i : i + 1], gram)
    sums_ref[0:MEMBERS, :] = gram
    sums_ref[MEMBERS:, :] = pltpu.roll(total, KP - len(PAIRS), 1)


def near(x):
    return pltpu.with_memory_space_constraint(x, VMEM)


def vmem(count):
    return [pl.BlockSpec(memory_space=VMEM)] * count


def smem(count):
    return [pl.BlockSpec(memory_space=SMEM)] * count


def on_device(
    initial_temp, land_mask, pert_table, pert_index, base_kh, member_mix, base_mix,
    owner, column, interp_w, obs_inv_var, observed,
):
    owners = ("lat", "lon")
    mem = lax.axis_index("mem").astype(jnp.int32).reshape(1)
    lat_at, lat_count = lax.axis_index("lat"), lax.axis_size("lat")
    lon_count = lax.axis_size("lon")
    w_t, iv_t, ob_t = interp_w.T, obs_inv_var.T, observed.T

    cells = jnp.transpose(initial_temp, (1, 2, 0)).astype(BF16)
    cells = jnp.concatenate(
        [
            cells,
            land_mask.astype(BF16)[:, :, None],
            jnp.zeros((CX, CY, KP - K - 1), BF16),
        ],
        2,
    )
    up = [(i, i + 1) for i in range(lat_count - 1)]
    down = [(i + 1, i) for i in range(lat_count - 1)]
    below = lax.ppermute(cells[:, CY - HALO :], "lat", up)
    above = lax.ppermute(cells[:, :HALO], "lat", down)
    below = jnp.where(lat_at == 0, cells[:, :HALO][:, ::-1], below)
    above = jnp.where(lat_at == lat_count - 1, cells[:, CY - HALO :][:, ::-1], above)
    tall = jnp.concatenate([below, cells, above], 1)

    def shift(x, by):
        return lax.ppermute(x, "lon", [(i, (i + by) % lon_count) for i in range(lon_count)])

    left2 = shift(cells[CX - 1 :], 2)
    right2 = shift(cells[:1], -2)
    left = shift(tall, 1)
    right = shift(tall, -1)

    send, code = pl.pallas_call(
        slots_kernel,
        out_shape=(VMEM((OWN * CAP, KP), BF16), VMEM((1, REC), jnp.int32)),
        in_specs=smem(1) + vmem(5),
        out_specs=tuple(vmem(2)),
        scratch_shapes=[VMEM((KP, REC), F32)],
        name="slots",
    )(mem, owner.reshape(1, REC), column.reshape(1, REC), w_t, iv_t, ob_t)
    recv = lax.all_to_all(
        send.reshape(OWN, CAP, KP), owners, split_axis=0, concat_axis=0, tiled=True
    )
    recv = recv.reshape(OWN * CAP, KP)

    fields, picks, base_rows = pl.pallas_call(
        window_kernel,
        out_shape=(
            VMEM((3, CX, K, CY), BF16),
            VMEM((CAP, OWN, 2 * KP), BF16),
            VMEM((OWN * CAP, KP), BF16),
        ),
        in_specs=smem(1) + vmem(10),
        out_specs=tuple(vmem(3)),
        scratch_shapes=[
            VMEM((14, ROWS + 16, KP), F32),
            VMEM((3, 14, ROWS + 16, KP), F32),
            VMEM((3, 14, ROWS + 16, KP), F32),
            VMEM((14, ROWS, KP), F32),
            VMEM((8, KP), F32),
            VMEM((2 * KP, 2 * KP), BF16),
            VMEM((2 * KP, 2 * KP), BF16),
            VMEM((KP, 2 * KP), BF16),
            VMEM((OWN * CAP, KP), F32),
            VMEM((OWN * CAP, KP), F32),
        ],
        name="window",
    )(
        pert_index, near(tall), near(left), near(right), near(left2), near(right2), near(recv),
        pert_table, base_kh.reshape(1, K), member_mix, base_mix,
    )

    members = lax.all_to_all(picks, "mem", split_axis=0, concat_axis=0, tiled=True)
    back = pl.pallas_call(
        functools.partial(gram_kernel, scale=1.0 / (OWN * REC * K)),
        out_shape=VMEM((OWN * CAP, KP), BF16),
        in_specs=smem(1) + vmem(3),
        out_specs=vmem(1)[0],
        scratch_shapes=[
            VMEM((OWN * CAP, KP), F32),
            VMEM((OWN * CAP, KP), F32),
            VMEM((MEMBERS, OWN, KP), F32),
            VMEM((MEMBERS, OWN, KP), F32),
            VMEM((KP, KP), F32),
        ],
        name="gram",
    )(mem, near(members), near(base_rows), near(recv))

    returned = lax.all_to_all(
        back.reshape(OWN, CAP, KP), owners, split_axis=0, concat_axis=0, tiled=True
    ).reshape(OWN * CAP, KP)
    misfit_t, sums = pl.pallas_call(
        result_kernel,
        out_shape=(
            jax.ShapeDtypeStruct((K, REC), F32),
            VMEM((2 * MEMBERS, KP), F32),
        ),
        in_specs=vmem(4),
        out_specs=tuple(vmem(2)),
        name="result",
    )(near(returned), near(code), w_t, ob_t)
    for pairs in (((0, 1), (2, 3)), ((0, 3), (1, 2))):
        sums = sums + lax.ppermute(sums, "mem", [p for a, b in pairs for p in ((a, b), (b, a))])
    gram, proj = sums[:MEMBERS, :MEMBERS], sums[MEMBERS, :MEMBERS]

    fields = jnp.transpose(fields, (0, 2, 1, 3))
    return fields[:2], fields[2], gram, proj, misfit_t.T


def solution(mesh):
    placed = (
        P(None, "lon", "lat"),
        P("lon", "lat"),
        P(),
        P("mem"),
        P(),
        P("mem", None, None),
        P(),
        P(("lat", "lon"), None),
        P(("lat", "lon")),
        P(("lat", "lon"), None),
        P(("lat", "lon"), None),
        P(("lat", "lon"), None),
    )
    return jax.shard_map(
        on_device,
        mesh=mesh,
        in_specs=placed,
        out_specs=(
            P("mem", None, "lon", "lat"),
            P(None, "lon", "lat"),
            P(),
            P(),
            P(("lat", "lon"), None),
        ),
        check_vma=False,
    )
```

```python
import functools

import jax
import jax.numpy as jnp
from jax import lax
from jax.experimental import pallas as pl
from jax.experimental.pallas import tpu as pltpu
from jax.sharding import PartitionSpec as P


STEPS = 5
BLOCK = (4, 5, 4, 6, 4)
K = 100
KP = 128
SPARE = KP - K
CX = 4
CY = 128
CAP = 4
OWN = 128
REC = 256
HALO = 8
ROWS = CY + 2 * HALO
COLS = CX * CY
MEMBERS = 8
PAIRS = [(a, b) for a in range(MEMBERS) for b in range(a, MEMBERS)]
F32 = jnp.float32
BF16 = jnp.bfloat16
NT = (((1,), (1,)), ((), ()))
NN = (((1,), (0,)), ((), ()))
TN = (((0,), (0,)), ((), ()))
SMEM = pltpu.SMEM
VMEM = pltpu.VMEM


def dot(a, b, dims):
    return lax.dot_general(a, b, dims, preferred_element_type=F32)


def ones_where(cond):
    return jnp.where(cond, 1.0, 0.0).astype(BF16)


def iota(shape, dim):
    return lax.broadcasted_iota(jnp.int32, shape, dim)


def slots_kernel(m_ref, owner_ref, column_ref, w_ref, iv_ref, ob_ref, out_ref, code_ref, pad):
    owner = owner_ref[...]
    column = column_ref[...]
    hit = iota((OWN, REC), 0) == owner
    before = ones_where(iota((REC, REC), 0) < iota((REC, REC), 1))
    earlier = dot(ones_where(hit), before, NN)
    rank = jnp.sum(jnp.where(hit, earlier, 0.0), 0, keepdims=True).astype(jnp.int32)
    slot = owner * CAP + rank
    code_ref[...] = slot
    mine = jnp.where(rank == m_ref[0], owner * CAP, -CAP)
    rows = iota((OWN * CAP, REC), 0)
    sub = iota((KP, REC), 0)
    high = (column // CY + 1).astype(F32)
    low = (column % CY).astype(F32)
    ids = jnp.where(sub == K, high, jnp.where(sub == K + 1, low, 0.0)).astype(BF16)
    placed = dot(ones_where(rows == slot), ids, NT)
    pad[...] = jnp.zeros((KP, REC), F32)
    for group, ref in enumerate((w_ref, iv_ref, ob_ref)):
        pad[0:K, :] = ref[...]
        placed += dot(ones_where(rows == mine + group), pad[...].astype(BF16), NT)
    out_ref[...] = placed.astype(BF16)


def window_kernel(
    index_ref, own_ref, left_ref, right_ref, left2_ref, right2_ref, recv_ref,
    table_ref, base_kh_ref, mix_ref, base_mix_ref,
    fields_ref, picks_ref, base_ref,
    start, ping, pong, ocean, kh_pad, mix_pad, one_pad, base_pad, first, second,
):
    body = pl.ds(8, ROWS)

    def fill(column, cells):
        cells = cells.astype(F32)
        start[column, body, :] = cells
        ocean[column] = jnp.broadcast_to(cells[:, K : K + 1], (ROWS, KP))

    start[0, pl.ds(16, CY), :] = left2_ref[0].astype(F32)
    start[13, pl.ds(16, CY), :] = right2_ref[0].astype(F32)
    for place, ref in ((1, left_ref), (5, own_ref), (9, right_ref)):
        for c in range(CX):
            fill(place + c, ref[c])
    kh_pad[...] = jnp.zeros((8, KP), F32)
    kh_pad[0:1, 0:K] = table_ref[pl.ds(index_ref[0], 1), :]
    kh_pad[1:2, 0:K] = table_ref[pl.ds(index_ref[1], 1), :]
    kh_pad[2:3, 0:K] = base_kh_ref[...]
    mix_pad[...] = jnp.zeros((2 * KP, 2 * KP), BF16)
    mix_pad[0:K, 0:K] = mix_ref[0]
    mix_pad[KP : KP + K, KP : KP + K] = mix_ref[1]
    same = iota((KP, KP), 0) == iota((KP, KP), 1)
    one_pad[...] = jnp.zeros((2 * KP, 2 * KP), BF16)
    one_pad[0:KP, 0:KP] = ones_where(same)
    one_pad[KP:, KP:] = ones_where(same)
    base_pad[...] = jnp.zeros((KP, 2 * KP), BF16)
    base_pad[0:K, 0:K] = base_mix_ref[...]
    base_pad[:, KP:] = ones_where(same)

    for step in range(STEPS):
        source, target = ((ping, pong), (pong, ping))[step % 2]
        row0, count = (8, ROWS) if step < STEPS - 1 else (16, CY)

        def advance(column, step=step, source=source, target=target, row0=row0, count=count):
            def at(run, lon, row):
                if step == 0:
                    return start[lon, pl.ds(row, count), :]
                return source[run, lon, pl.ds(row, count), :]

            def around(run):
                return (at(run, column + 1, row0) + at(run, column - 1, row0)) + (
                    at(run, column, row0 + 1) + at(run, column, row0 - 1)
                )

            values, rights = [], []
            shared = (at(0, column, row0), around(0)) if step == 0 else None
            for run in range(3):
                value, near = shared if step == 0 else (at(run, column, row0), around(run))
                kh = kh_pad[run : run + 1, :]
                values.append(value)
                rights.append((value * (1.0 - 4.0 * kh) + near * kh).astype(BF16))
            pair = jnp.concatenate(rights[:2], 1)
            both = dot(pair, mix_pad[...], NT) + dot(pair, one_pad[...], NT)
            twice = jnp.concatenate([rights[2], rights[2]], 1)
            mixed = (both[:, :KP], both[:, KP:], dot(twice, base_pad[...], NT))
            open_ = ocean[column, pl.ds(row0 - 8, count), :] > 0.0
            for run in range(3):
                new = jnp.where(open_, mixed[run], values[run])
                target[run, column, pl.ds(row0, count), :] = new.astype(BF16).astype(F32)

        columns = 12 - 2 * step
        block = BLOCK[step]

        def several(turn, _, step=step, block=block, advance=advance):
            for c in range(block):
                advance(step + 1 + turn * block + c)
            return 0

        if columns == block:
            several(0, 0)
        else:
            lax.fori_loop(0, columns // block, several, 0)

    final = pong
    flat = []
    for run in range(3):
        parts = []
        for c in range(CX):
            cells = final[run, 5 + c, pl.ds(16, CY), :]
            fields_ref[run, c] = cells.T[0:K, :].astype(BF16)
            parts.append(cells.astype(BF16))
        flat.append(jnp.concatenate(parts, 0))
    ids = recv_ref[...].astype(F32)
    at = ((ids[:, K : K + 1] - 1.0) * CY + ids[:, K + 1 : K + 2]).astype(jnp.int32)
    pick = ones_where(at == iota((OWN * CAP, COLS), 1))
    base_ref[...] = dot(pick, flat[2], NN).astype(BF16)
    both = dot(pick, jnp.concatenate(flat[:2], 1), NN)
    for half, scratch in enumerate((first, second)):
        scratch[...] = both[:, half * KP : (half + 1) * KP]
        for rank in range(CAP):
            picked = scratch[pl.ds(rank, OWN, stride=CAP), :]
            picks_ref[rank, :, half * KP : (half + 1) * KP] = picked.astype(BF16)


def gram_kernel(m_ref, recv_ref, base_ref, slot_ref, out_ref, slots, bases, greens, weighted, sums, *, scale):
    lane = iota((OWN, KP), 1)

    def deeper(x):
        return jnp.where(lane == K - 1, x, pltpu.roll(x, KP - 1, 1))

    slots[...] = slot_ref[...].astype(F32)
    weight = slots[pl.ds(0, OWN, stride=CAP), :]
    inv_var = jnp.where(lane < K, slots[pl.ds(1, OWN, stride=CAP), :], 0.0)
    measured = slots[pl.ds(2, OWN, stride=CAP), :]
    bases[...] = base_ref[...].astype(F32)
    base = bases[pl.ds(0, OWN, stride=CAP), :]
    for rank in range(1, CAP):
        base = jnp.where(m_ref[0] == rank, bases[pl.ds(rank, OWN, stride=CAP), :], base)

    def model(x):
        return weight * x + (1.0 - weight) * deeper(x)

    base_model = model(base)
    misfit = measured - base_model
    for member in range(MEMBERS):
        half = (member % 2) * KP
        picked = recv_ref[member // 2, :, half : half + KP].astype(F32)
        green = jnp.where(lane < K, model(picked) - base_model, 0.0).astype(BF16).astype(F32)
        greens[member] = green
        weighted[member] = green * inv_var
    sums[...] = jnp.zeros((KP, KP), F32)
    for i, (a, b) in enumerate(PAIRS):
        sums[i : i + 1, :] = jnp.sum(weighted[a] * greens[b], 0, keepdims=True)
    for a in range(MEMBERS):
        sums[len(PAIRS) + a : len(PAIRS) + a + 1, :] = jnp.sum(weighted[a] * misfit, 0, keepdims=True)
    total = jnp.sum(sums[...].T, 0, keepdims=True) * scale
    high = total.astype(BF16).astype(F32)
    high = jnp.broadcast_to(high, (8, KP))
    rest = jnp.broadcast_to(total, (8, KP)) - high
    turn = iota((8, KP), 0) % CAP
    tail = jnp.where(
        turn == 0,
        pltpu.roll(high, K, 1),
        jnp.where(
            turn == 1,
            pltpu.roll(high, K - SPARE, 1),
            jnp.where(turn == 2, pltpu.roll(rest, K, 1), pltpu.roll(rest, K - SPARE, 1)),
        ),
    )
    rows = bases[...].reshape(OWN * CAP // 8, 8, KP)
    rows = jnp.where(iota((1, 8, KP), 2) < K, rows, tail[None])
    out_ref[...] = rows.reshape(OWN * CAP, KP).astype(BF16)


def result_kernel(recv_ref, code_ref, w_ref, ob_ref, misfit_ref, sums_ref):
    recv = recv_ref[...]
    pick = ones_where(iota((OWN * CAP, REC), 0) == code_ref[...])
    picked = dot(recv, pick, TN)
    values = picked[0:K]
    deeper = jnp.concatenate([picked[1:K], picked[K - 1 : K]], 0)
    weight = w_ref[...]
    misfit_ref[...] = ob_ref[...] - (weight * values + (1.0 - weight) * deeper)
    part = jnp.sum(recv.astype(F32).reshape(OWN * CAP // 8, 8, KP), 0)
    part = part + pltpu.roll(part, 4, 0)
    part = part + pltpu.roll(part, 6, 0)
    sub, line = iota((8, KP), 0), iota((8, KP), 1)
    total = jnp.where(
        line < SPARE,
        pltpu.roll(jnp.broadcast_to(part[0:1], (8, KP)), SPARE, 1),
        pltpu.roll(jnp.broadcast_to(part[1:2], (8, KP)), 2 * SPARE, 1),
    )
    gram = jnp.zeros((8, KP), F32)
    for i, (a, b) in enumerate(PAIRS):
        here = ((sub == a) & (line == b)) | ((sub == b) & (line == a))
        gram = jnp.where(here, total[:, i : i + 1], gram)
    sums_ref[0:MEMBERS, :] = gram
    sums_ref[MEMBERS:, :] = pltpu.roll(total, KP - len(PAIRS), 1)


def near(x):
    return pltpu.with_memory_space_constraint(x, VMEM)


def vmem(count):
    return [pl.BlockSpec(memory_space=VMEM)] * count


def smem(count):
    return [pl.BlockSpec(memory_space=SMEM)] * count


def on_device(
    initial_temp, land_mask, pert_table, pert_index, base_kh, member_mix, base_mix,
    owner, column, interp_w, obs_inv_var, observed,
):
    owners = ("lat", "lon")
    mem = lax.axis_index("mem").astype(jnp.int32).reshape(1)
    lat_at, lat_count = lax.axis_index("lat"), lax.axis_size("lat")
    lon_count = lax.axis_size("lon")
    w_t, iv_t, ob_t = interp_w.T, obs_inv_var.T, observed.T

    cells = jnp.transpose(initial_temp, (1, 2, 0)).astype(BF16)
    cells = jnp.concatenate(
        [
            cells,
            land_mask.astype(BF16)[:, :, None],
            jnp.zeros((CX, CY, KP - K - 1), BF16),
        ],
        2,
    )
    up = [(i, i + 1) for i in range(lat_count - 1)]
    down = [(i + 1, i) for i in range(lat_count - 1)]
    below = lax.ppermute(cells[:, CY - HALO :], "lat", up)
    above = lax.ppermute(cells[:, :HALO], "lat", down)
    below = jnp.where(lat_at == 0, cells[:, :HALO][:, ::-1], below)
    above = jnp.where(lat_at == lat_count - 1, cells[:, CY - HALO :][:, ::-1], above)
    tall = jnp.concatenate([below, cells, above], 1)

    def shift(x, by):
        return lax.ppermute(x, "lon", [(i, (i + by) % lon_count) for i in range(lon_count)])

    left2 = shift(cells[CX - 1 :], 2)
    right2 = shift(cells[:1], -2)
    left = shift(tall, 1)
    right = shift(tall, -1)

    send, code = pl.pallas_call(
        slots_kernel,
        out_shape=(VMEM((OWN * CAP, KP), BF16), VMEM((1, REC), jnp.int32)),
        in_specs=smem(1) + vmem(5),
        out_specs=tuple(vmem(2)),
        scratch_shapes=[VMEM((KP, REC), F32)],
        name="slots",
    )(mem, owner.reshape(1, REC), column.reshape(1, REC), w_t, iv_t, ob_t)
    recv = lax.all_to_all(
        send.reshape(OWN, CAP, KP), owners, split_axis=0, concat_axis=0, tiled=True
    )
    recv = recv.reshape(OWN * CAP, KP)

    fields, picks, base_rows = pl.pallas_call(
        window_kernel,
        out_shape=(
            VMEM((3, CX, K, CY), BF16),
            VMEM((CAP, OWN, 2 * KP), BF16),
            VMEM((OWN * CAP, KP), BF16),
        ),
        in_specs=smem(1) + vmem(10),
        out_specs=tuple(vmem(3)),
        scratch_shapes=[
            VMEM((14, ROWS + 16, KP), F32),
            VMEM((3, 14, ROWS + 16, KP), F32),
            VMEM((3, 14, ROWS + 16, KP), F32),
            VMEM((14, ROWS, KP), F32),
            VMEM((8, KP), F32),
            VMEM((2 * KP, 2 * KP), BF16),
            VMEM((2 * KP, 2 * KP), BF16),
            VMEM((KP, 2 * KP), BF16),
            VMEM((OWN * CAP, KP), F32),
            VMEM((OWN * CAP, KP), F32),
        ],
        name="window",
    )(
        pert_index, near(tall), near(left), near(right), near(left2), near(right2), near(recv),
        pert_table, base_kh.reshape(1, K), member_mix, base_mix,
    )

    members = lax.all_to_all(picks, "mem", split_axis=0, concat_axis=0, tiled=True)
    member_temp = jnp.transpose(fields[:2], (0, 2, 1, 3))
    base_temp = jnp.transpose(fields[2], (1, 0, 2))
    back = pl.pallas_call(
        functools.partial(gram_kernel, scale=1.0 / (OWN * REC * K)),
        out_shape=VMEM((OWN * CAP, KP), BF16),
        in_specs=smem(1) + vmem(3),
        out_specs=vmem(1)[0],
        scratch_shapes=[
            VMEM((OWN * CAP, KP), F32),
            VMEM((OWN * CAP, KP), F32),
            VMEM((MEMBERS, OWN, KP), F32),
            VMEM((MEMBERS, OWN, KP), F32),
            VMEM((KP, KP), F32),
        ],
        name="gram",
    )(mem, near(members), near(base_rows), near(recv))

    returned = lax.all_to_all(
        back.reshape(OWN, CAP, KP), owners, split_axis=0, concat_axis=0, tiled=True
    )
    returned = returned.reshape(OWN * CAP, KP)
    misfit_t, sums = pl.pallas_call(
        result_kernel,
        out_shape=(
            jax.ShapeDtypeStruct((K, REC), F32),
            VMEM((2 * MEMBERS, KP), F32),
        ),
        in_specs=vmem(4),
        out_specs=tuple(vmem(2)),
        name="result",
    )(near(returned), near(code), w_t, ob_t)
    for pairs in (((0, 1), (2, 3)), ((0, 3), (1, 2))):
        sums = sums + lax.ppermute(sums, "mem", [p for a, b in pairs for p in ((a, b), (b, a))])
    gram, proj = sums[:MEMBERS, :MEMBERS], sums[MEMBERS, :MEMBERS]

    return member_temp, base_temp, gram, proj, misfit_t.T


def solution(mesh):
    placed = (
        P(None, "lon", "lat"),
        P("lon", "lat"),
        P(),
        P("mem"),
        P(),
        P("mem", None, None),
        P(),
        P(("lat", "lon"), None),
        P(("lat", "lon")),
        P(("lat", "lon"), None),
        P(("lat", "lon"), None),
        P(("lat", "lon"), None),
    )
    return jax.shard_map(
        on_device,
        mesh=mesh,
        in_specs=placed,
        out_specs=(
            P("mem", None, "lon", "lat"),
            P(None, "lon", "lat"),
            P(),
            P(),
            P(("lat", "lon"), None),
        ),
        check_vma=False,
    )
```

```python
import functools

import jax
import jax.numpy as jnp
from jax import lax
from jax.experimental import pallas as pl
from jax.experimental.pallas import tpu as pltpu
from jax.sharding import PartitionSpec as P


STEPS = 5
BLOCK = 2
K = 100
KP = 128
SPARE = KP - K
CX = 4
CY = 128
CAP = 4
OWN = 128
REC = 256
HALO = 8
ROWS = CY + 2 * HALO
COLS = CX * CY
MEMBERS = 8
RUNS = MEMBERS + 1
MIX = 104
PAIRS = [(a, b) for a in range(MEMBERS) for b in range(a, MEMBERS)]
F32 = jnp.float32
BF16 = jnp.bfloat16
NT = (((1,), (1,)), ((), ()))
NN = (((1,), (0,)), ((), ()))
TN = (((0,), (0,)), ((), ()))
SMEM = pltpu.SMEM
VMEM = pltpu.VMEM


def dot(a, b, dims):
    return lax.dot_general(a, b, dims, preferred_element_type=F32)


def ones_where(cond):
    return jnp.where(cond, 1.0, 0.0).astype(BF16)


def iota(shape, dim):
    return lax.broadcasted_iota(jnp.int32, shape, dim)


def slots_kernel(owner_ref, column_ref, w_ref, iv_ref, ob_ref, out_ref, code_ref, pad, rows3):
    owner = owner_ref[...]
    column = column_ref[...]
    hit = iota((OWN, REC), 0) == owner
    before = ones_where(iota((REC, REC), 0) < iota((REC, REC), 1))
    earlier = dot(ones_where(hit), before, NN)
    rank = jnp.sum(jnp.where(hit, earlier, 0.0), 0, keepdims=True).astype(jnp.int32)
    slot = owner * CAP + rank
    code_ref[...] = slot
    pad[...] = jnp.zeros((3 * KP, REC), F32)
    for group, ref in enumerate((w_ref, iv_ref, ob_ref)):
        pad[group * KP : group * KP + K, :] = ref[...]
    pad[K : K + 1, :] = (column // CY + 1).astype(F32)
    pad[K + 1 : K + 2, :] = (column % CY).astype(F32)
    place = ones_where(iota((OWN * CAP, REC), 0) == slot)
    placed = dot(place, pad[...].astype(BF16), NT)
    for group in range(3):
        rows3[pl.ds(group, OWN * CAP, stride=3), :] = placed[:, group * KP : (group + 1) * KP]
    out_ref[...] = rows3[...].astype(BF16)


def mixes_kernel(index_ref, table_ref, mix_ref, out_ref, pad):
    for j in range(2):
        pad[...] = jnp.zeros((MIX, KP), F32)
        pad[0:K, 0:K] = mix_ref[j].astype(F32)
        kh = table_ref[pl.ds(index_ref[j], 1), :]
        high = kh.astype(BF16).astype(F32)
        pad[K : K + 1, 0:K] = high
        pad[K + 1 : K + 2, 0:K] = kh - high
        out_ref[j] = pad[...].astype(BF16)


def window_kernel(
    m_ref, own_ref, left_ref, right_ref, left2_ref, right2_ref, recv_ref,
    mixes0_ref, mixes1_ref, mixes2_ref, mixes3_ref,
    base_kh_ref, base_mix_ref,
    fields_ref, out_ref,
    start, ping, pong, ocean, kh_pad, mix_pad, one_pad, base_pad, slots, greens, weighted, sums,
    *, scale,
):
    body = pl.ds(8, ROWS)

    def fill(column, cells):
        cells = cells.astype(F32)
        start[column, body, :] = cells
        ocean[column] = jnp.broadcast_to(cells[:, K : K + 1], (ROWS, KP))

    start[0, pl.ds(16, CY), :] = left2_ref[0].astype(F32)
    start[13, pl.ds(16, CY), :] = right2_ref[0].astype(F32)
    for place, ref in ((1, left_ref), (5, own_ref), (9, right_ref)):
        for c in range(CX):
            fill(place + c, ref[c])
    kh_pad[...] = jnp.zeros((16, KP), F32)
    mix_pad[...] = jnp.zeros((MEMBERS // 2, 2 * KP, 2 * KP), BF16)
    for back, ref in enumerate((mixes0_ref, mixes1_ref, mixes2_ref, mixes3_ref)):
        pair = lax.rem(m_ref[0] + 4 - back, 4)
        for half in range(2):
            spot = half * KP
            mix_pad[pair, spot : spot + K, spot : spot + KP] = ref[half, 0:K, :]
            parts = ref[half, MIX - 8 : MIX, :].astype(F32)
            kh_pad[pl.ds(2 * pair + half, 1), :] = parts[4:5] + parts[5:6]
    kh_pad[MEMBERS : MEMBERS + 1, 0:K] = base_kh_ref[...]
    same = iota((KP, KP), 0) == iota((KP, KP), 1)
    one_pad[...] = jnp.zeros((2 * KP, 2 * KP), BF16)
    one_pad[0:KP, 0:KP] = ones_where(same)
    one_pad[KP:, KP:] = ones_where(same)
    base_pad[...] = jnp.zeros((KP, 2 * KP), BF16)
    base_pad[0:K, 0:K] = base_mix_ref[...]
    base_pad[:, KP:] = ones_where(same)

    for step in range(STEPS):
        source, target = ((ping, pong), (pong, ping))[step % 2]
        row0, count = (12, CY + 8) if step < STEPS - 1 else (16, CY)

        def advance(column, step=step, source=source, target=target, row0=row0, count=count):
            def at(run, lon, row):
                if step == 0:
                    return start[lon, pl.ds(row, count), :]
                return source[run, lon, pl.ds(row, count), :]

            def around(run):
                return (at(run, column + 1, row0) + at(run, column - 1, row0)) + (
                    at(run, column, row0 + 1) + at(run, column, row0 - 1)
                )

            shared = (at(0, column, row0), around(0)) if step == 0 else None
            open_ = ocean[column, pl.ds(row0 - 8, count), :] > 0.0

            def right_of(run):
                value, near = shared if step == 0 else (at(run, column, row0), around(run))
                kh = kh_pad[run : run + 1, :]
                return value, (value * (1.0 - 4.0 * kh) + near * kh).astype(BF16)

            def put(run, mixed, value):
                new = jnp.where(open_, mixed, value)
                target[run, column, pl.ds(row0, count), :] = new.astype(BF16).astype(F32)

            for pair in range(MEMBERS // 2):
                value0, right0 = right_of(2 * pair)
                value1, right1 = right_of(2 * pair + 1)
                right = jnp.concatenate([right0, right1], 1)
                both = dot(right, mix_pad[pair], NT) + dot(right, one_pad[...], NT)
                put(2 * pair, both[:, :KP], value0)
                put(2 * pair + 1, both[:, KP:], value1)
            value, right = right_of(MEMBERS)
            put(MEMBERS, dot(jnp.concatenate([right, right], 1), base_pad[...], NT), value)

        columns = 12 - 2 * step

        def several(turn, _, step=step, advance=advance):
            for c in range(BLOCK):
                advance(step + 1 + turn * BLOCK + c)
            return 0

        lax.fori_loop(0, columns // BLOCK, several, 0)

    final = pong

    def flat(run):
        return jnp.concatenate([final[run, 5 + c, pl.ds(16, CY), :].astype(BF16) for c in range(CX)], 0)

    for place, run in enumerate((2 * m_ref[0], 2 * m_ref[0] + 1, MEMBERS)):
        for c in range(CX):
            fields_ref[place, c] = final[run, 5 + c, pl.ds(16, CY), :].T[0:K, :].astype(BF16)

    count = OWN * CAP
    slots[...] = recv_ref[...].astype(F32)
    weight = slots[pl.ds(0, count, stride=3), :]
    inv_var = slots[pl.ds(1, count, stride=3), :]
    measured = slots[pl.ds(2, count, stride=3), :]
    at = ((weight[:, K : K + 1] - 1.0) * CY + weight[:, K + 1 : K + 2]).astype(jnp.int32)
    pick = ones_where(at == iota((count, COLS), 1))
    weight = jnp.where(iota((count, KP), 1) < K - 1, weight, 1.0)

    def model(x):
        below = pltpu.roll(x, KP - 1, 1)
        return below + weight * (x - below)

    base = dot(pick, flat(MEMBERS), NN)
    misfit = measured - model(base)
    for pair in range(MEMBERS // 2):
        both = dot(pick, jnp.concatenate([flat(2 * pair), flat(2 * pair + 1)], 1), NN)
        for half in range(2):
            green = model(both[:, half * KP : (half + 1) * KP] - base).astype(BF16).astype(F32)
            greens[2 * pair + half] = green
            weighted[2 * pair + half] = green * inv_var
    sums[...] = jnp.zeros((KP, KP), F32)
    for i, (a, b) in enumerate(PAIRS):
        sums[i : i + 1, :] = jnp.sum(weighted[a] * greens[b], 0, keepdims=True)
    for a in range(MEMBERS):
        sums[len(PAIRS) + a : len(PAIRS) + a + 1, :] = jnp.sum(weighted[a] * misfit, 0, keepdims=True)
    total = jnp.sum(sums[...].T, 0, keepdims=True) * scale
    high = jnp.broadcast_to(total.astype(BF16).astype(F32), (8, KP))
    rest = jnp.broadcast_to(total, (8, KP)) - high
    turn = iota((8, KP), 0) % CAP
    tail = jnp.where(
        turn == 0,
        pltpu.roll(high, K, 1),
        jnp.where(
            turn == 1,
            pltpu.roll(high, K - SPARE, 1),
            jnp.where(turn == 2, pltpu.roll(rest, K, 1), pltpu.roll(rest, K - SPARE, 1)),
        ),
    )
    rows = jnp.where(iota((1, 8, KP), 2) < K, base.reshape(count // 8, 8, KP), tail[None])
    out_ref[...] = rows.reshape(count, KP).astype(BF16)


def result_kernel(recv_ref, code_ref, w_ref, ob_ref, misfit_ref, gram_ref, proj_ref):
    recv = recv_ref[...]
    pick = ones_where(iota((OWN * CAP, REC), 0) == code_ref[...])
    picked = dot(recv, pick, TN)
    values = picked[0:K]
    deeper = jnp.concatenate([picked[1:K], picked[K - 1 : K]], 0)
    weight = w_ref[...]
    misfit_ref[...] = ob_ref[...] - (weight * values + (1.0 - weight) * deeper)
    part = jnp.sum(recv.astype(F32).reshape(OWN * CAP // 8, 8, KP), 0)
    part = part + pltpu.roll(part, 4, 0)
    part = part + pltpu.roll(part, 6, 0)
    sub, line = iota((8, KP), 0), iota((8, KP), 1)
    total = jnp.where(
        line < SPARE,
        pltpu.roll(jnp.broadcast_to(part[0:1], (8, KP)), SPARE, 1),
        pltpu.roll(jnp.broadcast_to(part[1:2], (8, KP)), 2 * SPARE, 1),
    )
    gram = jnp.zeros((8, KP), F32)
    for i, (a, b) in enumerate(PAIRS):
        here = ((sub == a) & (line == b)) | ((sub == b) & (line == a))
        gram = jnp.where(here, total[:, i : i + 1], gram)
    gram_ref[...] = gram[:, 0:MEMBERS]
    proj_ref[...] = pltpu.roll(total, KP - len(PAIRS), 1)[0:1, 0:MEMBERS]


def near(x):
    return pltpu.with_memory_space_constraint(x, VMEM)


def vmem(count):
    return [pl.BlockSpec(memory_space=VMEM)] * count


def smem(count):
    return [pl.BlockSpec(memory_space=SMEM)] * count


def on_device(
    initial_temp, land_mask, pert_table, pert_index, base_kh, member_mix, base_mix,
    owner, column, interp_w, obs_inv_var, observed,
):
    owners = ("lat", "lon")
    mem = lax.axis_index("mem").astype(jnp.int32).reshape(1)
    lat_at, lat_count = lax.axis_index("lat"), lax.axis_size("lat")
    lon_count = lax.axis_size("lon")
    w_t, iv_t, ob_t = interp_w.T, obs_inv_var.T, observed.T

    cells = jnp.transpose(initial_temp, (1, 2, 0)).astype(BF16)
    cells = jnp.concatenate(
        [
            cells,
            land_mask.astype(BF16)[:, :, None],
            jnp.zeros((CX, CY, KP - K - 1), BF16),
        ],
        2,
    )
    up = [(i, i + 1) for i in range(lat_count - 1)]
    down = [(i + 1, i) for i in range(lat_count - 1)]
    below = lax.ppermute(cells[:, CY - HALO :], "lat", up)
    above = lax.ppermute(cells[:, :HALO], "lat", down)
    below = jnp.where(lat_at == 0, cells[:, :HALO][:, ::-1], below)
    above = jnp.where(lat_at == lat_count - 1, cells[:, CY - HALO :][:, ::-1], above)
    tall = jnp.concatenate([below, cells, above], 1)

    def shift(x, by):
        return lax.ppermute(x, "lon", [(i, (i + by) % lon_count) for i in range(lon_count)])

    left2 = shift(cells[CX - 1 :], 2)
    right2 = shift(cells[:1], -2)
    left = shift(tall, 1)
    right = shift(tall, -1)

    send, code = pl.pallas_call(
        slots_kernel,
        out_shape=(VMEM((3 * OWN * CAP, KP), BF16), VMEM((1, REC), jnp.int32)),
        in_specs=vmem(5),
        out_specs=tuple(vmem(2)),
        scratch_shapes=[VMEM((3 * KP, REC), F32), VMEM((3 * OWN * CAP, KP), F32)],
        name="slots",
    )(owner.reshape(1, REC), column.reshape(1, REC), w_t, iv_t, ob_t)
    recv = lax.all_to_all(
        send.reshape(OWN, 3, CAP, KP), owners, split_axis=0, concat_axis=0, tiled=True
    )
    recv = recv.reshape(3 * OWN * CAP, KP)

    own_mixes = pl.pallas_call(
        mixes_kernel,
        out_shape=VMEM((2, MIX, KP), BF16),
        in_specs=smem(1) + vmem(2),
        out_specs=vmem(1)[0],
        scratch_shapes=[VMEM((MIX, KP), F32)],
        name="mixes",
    )(pert_index, pert_table, member_mix)
    mixes = [own_mixes]
    for back in range(1, 4):
        mixes.append(lax.ppermute(own_mixes, "mem", [(i, (i + back) % 4) for i in range(4)]))

    fields, back = pl.pallas_call(
        functools.partial(window_kernel, scale=1.0 / (OWN * REC * K)),
        out_shape=(VMEM((3, CX, K, CY), BF16), VMEM((OWN * CAP, KP), BF16)),
        in_specs=smem(1) + vmem(12),
        out_specs=tuple(vmem(2)),
        scratch_shapes=[
            VMEM((14, ROWS + 16, KP), F32),
            VMEM((RUNS, 14, ROWS + 16, KP), F32),
            VMEM((RUNS, 14, ROWS + 16, KP), F32),
            VMEM((14, ROWS, KP), F32),
            VMEM((16, KP), F32),
            VMEM((MEMBERS // 2, 2 * KP, 2 * KP), BF16),
            VMEM((2 * KP, 2 * KP), BF16),
            VMEM((KP, 2 * KP), BF16),
            VMEM((3 * OWN * CAP, KP), F32),
            VMEM((MEMBERS, OWN * CAP, KP), F32),
            VMEM((MEMBERS, OWN * CAP, KP), F32),
            VMEM((KP, KP), F32),
        ],
        name="window",
    )(
        mem, near(tall), near(left), near(right), near(left2), near(right2), near(recv),
        *map(near, mixes),
        base_kh.reshape(1, K), base_mix,
    )

    returned = lax.all_to_all(
        back.reshape(OWN, CAP, KP), owners, split_axis=0, concat_axis=0, tiled=True
    )
    returned = returned.reshape(OWN * CAP, KP)
    misfit_t, gram, proj = pl.pallas_call(
        result_kernel,
        out_shape=(
            jax.ShapeDtypeStruct((K, REC), F32),
            jax.ShapeDtypeStruct((MEMBERS, MEMBERS), F32),
            jax.ShapeDtypeStruct((1, MEMBERS), F32),
        ),
        in_specs=vmem(4),
        out_specs=tuple(vmem(3)),
        name="result",
    )(near(returned), near(code), w_t, ob_t)
    proj = proj.reshape(MEMBERS)
    fields = jnp.transpose(fields, (0, 2, 1, 3))
    member_temp, base_temp = fields[:2], fields[2]

    return member_temp, base_temp, gram, proj, misfit_t.T


def solution(mesh):
    placed = (
        P(None, "lon", "lat"),
        P("lon", "lat"),
        P(),
        P("mem"),
        P(),
        P("mem", None, None),
        P(),
        P(("lat", "lon"), None),
        P(("lat", "lon")),
        P(("lat", "lon"), None),
        P(("lat", "lon"), None),
        P(("lat", "lon"), None),
    )
    return jax.shard_map(
        on_device,
        mesh=mesh,
        in_specs=placed,
        out_specs=(
            P("mem", None, "lon", "lat"),
            P(None, "lon", "lat"),
            P(),
            P(),
            P(("lat", "lon"), None),
        ),
        check_vma=False,
    )
```

```python
import functools

import jax
import jax.numpy as jnp
from jax import lax
from jax.experimental import pallas as pl
from jax.experimental.pallas import tpu as pltpu
from jax.sharding import PartitionSpec as P


STEPS = 5
BLOCK = 2
K = 100
KP = 128
SPARE = KP - K
CX = 4
CY = 128
CAP = 4
OWN = 128
REC = 256
HALO = 8
ROWS = CY + 2 * HALO
COLS = CX * CY
MEMBERS = 8
RUNS = MEMBERS + 1
MIX = 104
PAIRS = [(a, b) for a in range(MEMBERS) for b in range(a, MEMBERS)]
F32 = jnp.float32
BF16 = jnp.bfloat16
NT = (((1,), (1,)), ((), ()))
NN = (((1,), (0,)), ((), ()))
TN = (((0,), (0,)), ((), ()))
SMEM = pltpu.SMEM
VMEM = pltpu.VMEM


def dot(a, b, dims):
    return lax.dot_general(a, b, dims, preferred_element_type=F32)


def ones_where(cond):
    return jnp.where(cond, 1.0, 0.0).astype(BF16)


def iota(shape, dim):
    return lax.broadcasted_iota(jnp.int32, shape, dim)


def slots_kernel(owner_ref, column_ref, w_ref, iv_ref, ob_ref, out_ref, code_ref, pad, rows3):
    owner = owner_ref[...]
    column = column_ref[...]
    hit = iota((OWN, REC), 0) == owner
    before = ones_where(iota((REC, REC), 0) < iota((REC, REC), 1))
    earlier = dot(ones_where(hit), before, NN)
    rank = jnp.sum(jnp.where(hit, earlier, 0.0), 0, keepdims=True).astype(jnp.int32)
    slot = owner * CAP + rank
    code_ref[...] = slot
    pad[...] = jnp.zeros((3 * KP, REC), F32)
    for group, ref in enumerate((w_ref, iv_ref, ob_ref)):
        pad[group * KP : group * KP + K, :] = ref[...]
    pad[K : K + 1, :] = (column // CY + 1).astype(F32)
    pad[K + 1 : K + 2, :] = (column % CY).astype(F32)
    place = ones_where(iota((OWN * CAP, REC), 0) == slot)
    placed = dot(place, pad[...].astype(BF16), NT)
    for group in range(3):
        rows3[pl.ds(group, OWN * CAP, stride=3), :] = placed[:, group * KP : (group + 1) * KP]
    out_ref[...] = rows3[...].astype(BF16)


def mixes_kernel(index_ref, table_ref, mix_ref, out_ref, pad):
    for j in range(2):
        pad[...] = jnp.zeros((MIX, KP), F32)
        pad[0:K, 0:K] = mix_ref[j].astype(F32)
        kh = table_ref[pl.ds(index_ref[j], 1), :]
        high = kh.astype(BF16).astype(F32)
        pad[K : K + 1, 0:K] = high
        pad[K + 1 : K + 2, 0:K] = kh - high
        out_ref[j] = pad[...].astype(BF16)


def window_kernel(
    m_ref, lon_ref, own_ref, near0_ref, near1_ref, far0_ref, far1_ref, recv_ref,
    mixes0_ref, mixes1_ref, mixes2_ref, mixes3_ref,
    base_kh_ref, base_mix_ref,
    fields_ref, out_ref,
    start, ping, pong, ocean, kh_pad, mix_pad, one_pad, base_pad, slots, greens, weighted, sums,
    *, scale,
):
    body = pl.ds(8, ROWS)

    def fill(column, cells):
        cells = cells.astype(F32)
        start[column, body, :] = cells
        ocean[column] = jnp.broadcast_to(cells[:, K : K + 1], (ROWS, KP))

    near_side = 1 - lax.rem(lon_ref[0], 2)
    far_side = 1 - lax.rem(lon_ref[0] // 2, 2)
    start[13 * far_side, pl.ds(16, CY), :] = far0_ref[0].astype(F32)
    start[13 * (1 - far_side), pl.ds(16, CY), :] = far1_ref[0].astype(F32)
    for c in range(CX):
        fill(5 + c, own_ref[c])
        fill(1 + 8 * near_side + c, near0_ref[c])
        fill(1 + 8 * (1 - near_side) + c, near1_ref[c])
    kh_pad[...] = jnp.zeros((16, KP), F32)
    mix_pad[...] = jnp.zeros((MEMBERS // 2, 2 * KP, 2 * KP), BF16)
    turned = lax.rem(m_ref[0] + 2, 4)
    sources = (m_ref[0], m_ref[0] + 1 - 2 * lax.rem(m_ref[0], 2), 3 - m_ref[0], turned)
    for pair, ref in zip(sources, (mixes0_ref, mixes1_ref, mixes2_ref, mixes3_ref)):
        for half in range(2):
            spot = half * KP
            mix_pad[pair, spot : spot + K, spot : spot + KP] = ref[half, 0:K, :]
            parts = ref[half, MIX - 8 : MIX, :].astype(F32)
            kh_pad[pl.ds(2 * pair + half, 1), :] = parts[4:5] + parts[5:6]
    kh_pad[MEMBERS : MEMBERS + 1, 0:K] = base_kh_ref[...]
    same = iota((KP, KP), 0) == iota((KP, KP), 1)
    one_pad[...] = jnp.zeros((2 * KP, 2 * KP), BF16)
    one_pad[0:KP, 0:KP] = ones_where(same)
    one_pad[KP:, KP:] = ones_where(same)
    base_pad[...] = jnp.zeros((KP, 2 * KP), BF16)
    base_pad[0:K, 0:K] = base_mix_ref[...]
    base_pad[:, KP:] = ones_where(same)

    for step in range(STEPS):
        source, target = ((ping, pong), (pong, ping))[step % 2]
        row0, count = (12, CY + 8) if step < STEPS - 1 else (16, CY)

        def advance(column, step=step, source=source, target=target, row0=row0, count=count):
            def at(run, lon, row):
                if step == 0:
                    return start[lon, pl.ds(row, count), :]
                return source[run, lon, pl.ds(row, count), :]

            def around(run):
                return (at(run, column + 1, row0) + at(run, column - 1, row0)) + (
                    at(run, column, row0 + 1) + at(run, column, row0 - 1)
                )

            shared = (at(0, column, row0), around(0)) if step == 0 else None
            open_ = ocean[column, pl.ds(row0 - 8, count), :] > 0.0

            def right_of(run):
                value, near = shared if step == 0 else (at(run, column, row0), around(run))
                kh = kh_pad[run : run + 1, :]
                return value, (value * (1.0 - 4.0 * kh) + near * kh).astype(BF16)

            def put(run, mixed, value):
                new = jnp.where(open_, mixed, value)
                target[run, column, pl.ds(row0, count), :] = new.astype(BF16).astype(F32)

            for pair in range(MEMBERS // 2):
                value0, right0 = right_of(2 * pair)
                value1, right1 = right_of(2 * pair + 1)
                right = jnp.concatenate([right0, right1], 1)
                both = dot(right, mix_pad[pair], NT) + dot(right, one_pad[...], NT)
                put(2 * pair, both[:, :KP], value0)
                put(2 * pair + 1, both[:, KP:], value1)
            value, right = right_of(MEMBERS)
            put(MEMBERS, dot(jnp.concatenate([right, right], 1), base_pad[...], NT), value)

        columns = 12 - 2 * step

        def several(turn, _, step=step, advance=advance):
            for c in range(BLOCK):
                advance(step + 1 + turn * BLOCK + c)
            return 0

        lax.fori_loop(0, columns // BLOCK, several, 0)

    final = pong

    def flat(run):
        return jnp.concatenate([final[run, 5 + c, pl.ds(16, CY), :].astype(BF16) for c in range(CX)], 0)

    for place, run in enumerate((2 * m_ref[0], 2 * m_ref[0] + 1, MEMBERS)):
        for c in range(CX):
            fields_ref[place, c] = final[run, 5 + c, pl.ds(16, CY), :].T[0:K, :].astype(BF16)

    count = OWN * CAP
    slots[...] = recv_ref[...].astype(F32)
    weight = slots[pl.ds(0, count, stride=3), :]
    inv_var = slots[pl.ds(1, count, stride=3), :]
    measured = slots[pl.ds(2, count, stride=3), :]
    at = ((weight[:, K : K + 1] - 1.0) * CY + weight[:, K + 1 : K + 2]).astype(jnp.int32)
    pick = ones_where(at == iota((count, COLS), 1))
    weight = jnp.where(iota((count, KP), 1) < K - 1, weight, 1.0)

    def model(x):
        below = pltpu.roll(x, KP - 1, 1)
        return below + weight * (x - below)

    base = dot(pick, flat(MEMBERS), NN)
    misfit = measured - model(base)
    for pair in range(MEMBERS // 2):
        both = dot(pick, jnp.concatenate([flat(2 * pair), flat(2 * pair + 1)], 1), NN)
        for half in range(2):
            green = model(both[:, half * KP : (half + 1) * KP] - base).astype(BF16).astype(F32)
            greens[2 * pair + half] = green
            weighted[2 * pair + half] = green * inv_var
    sums[...] = jnp.zeros((KP, KP), F32)
    for i, (a, b) in enumerate(PAIRS):
        sums[i : i + 1, :] = jnp.sum(weighted[a] * greens[b], 0, keepdims=True)
    for a in range(MEMBERS):
        sums[len(PAIRS) + a : len(PAIRS) + a + 1, :] = jnp.sum(weighted[a] * misfit, 0, keepdims=True)
    total = jnp.sum(sums[...].T, 0, keepdims=True) * scale
    high = jnp.broadcast_to(total.astype(BF16).astype(F32), (8, KP))
    rest = jnp.broadcast_to(total, (8, KP)) - high
    turn = iota((8, KP), 0) % CAP
    tail = jnp.where(
        turn == 0,
        pltpu.roll(high, K, 1),
        jnp.where(
            turn == 1,
            pltpu.roll(high, K - SPARE, 1),
            jnp.where(turn == 2, pltpu.roll(rest, K, 1), pltpu.roll(rest, K - SPARE, 1)),
        ),
    )
    rows = jnp.where(iota((1, 8, KP), 2) < K, base.reshape(count // 8, 8, KP), tail[None])
    out_ref[...] = rows.reshape(count, KP).astype(BF16)


def result_kernel(recv_ref, code_ref, w_ref, ob_ref, misfit_ref, gram_ref, proj_ref):
    recv = recv_ref[...]
    pick = ones_where(iota((OWN * CAP, REC), 0) == code_ref[...])
    picked = dot(recv, pick, TN)
    values = picked[0:K]
    deeper = jnp.concatenate([picked[1:K], picked[K - 1 : K]], 0)
    weight = w_ref[...]
    misfit_ref[...] = ob_ref[...] - (weight * values + (1.0 - weight) * deeper)
    part = jnp.sum(recv.astype(F32).reshape(OWN * CAP // 8, 8, KP), 0)
    part = part + pltpu.roll(part, 4, 0)
    part = part + pltpu.roll(part, 6, 0)
    sub, line = iota((8, KP), 0), iota((8, KP), 1)
    total = jnp.where(
        line < SPARE,
        pltpu.roll(jnp.broadcast_to(part[0:1], (8, KP)), SPARE, 1),
        pltpu.roll(jnp.broadcast_to(part[1:2], (8, KP)), 2 * SPARE, 1),
    )
    gram = jnp.zeros((8, KP), F32)
    for i, (a, b) in enumerate(PAIRS):
        here = ((sub == a) & (line == b)) | ((sub == b) & (line == a))
        gram = jnp.where(here, total[:, i : i + 1], gram)
    gram_ref[...] = gram[:, 0:MEMBERS]
    proj_ref[...] = pltpu.roll(total, KP - len(PAIRS), 1)[0:1, 0:MEMBERS]


def near(x):
    return pltpu.with_memory_space_constraint(x, VMEM)


def vmem(count):
    return [pl.BlockSpec(memory_space=VMEM)] * count


def smem(count):
    return [pl.BlockSpec(memory_space=SMEM)] * count


def on_device(
    initial_temp, land_mask, pert_table, pert_index, base_kh, member_mix, base_mix,
    owner, column, interp_w, obs_inv_var, observed,
):
    owners = ("lat", "lon")
    mem = lax.axis_index("mem").astype(jnp.int32).reshape(1)
    lat_at, lat_count = lax.axis_index("lat"), lax.axis_size("lat")
    lon_count = lax.axis_size("lon")
    w_t, iv_t, ob_t = interp_w.T, obs_inv_var.T, observed.T

    cells = jnp.transpose(initial_temp, (1, 2, 0)).astype(BF16)
    cells = jnp.concatenate(
        [
            cells,
            land_mask.astype(BF16)[:, :, None],
            jnp.zeros((CX, CY, KP - K - 1), BF16),
        ],
        2,
    )
    low, top = cells[:, :HALO], cells[:, CY - HALO :]
    even = lat_at % 2 == 0
    inner = [p for i in range(1, lat_count - 1, 2) for p in ((i, i + 1), (i + 1, i))]
    outer = [p for i in range(0, lat_count, 2) for p in ((i, i + 1), (i + 1, i))]
    at_inner = lax.ppermute(jnp.where(even, low, top), "lat", inner)
    at_outer = lax.ppermute(jnp.where(even, top, low), "lat", outer)
    at_inner = jnp.where(lat_at == 0, low[:, ::-1], at_inner)
    at_inner = jnp.where(lat_at == lat_count - 1, top[:, ::-1], at_inner)
    below, above = jnp.where(even, at_inner, at_outer), jnp.where(even, at_outer, at_inner)
    tall = jnp.concatenate([below, cells, above], 1)

    def swap(x, first, by):
        left = [i for i in range(lon_count) if (i // by) % 2 == first]
        pairs = [(i, (i + by) % lon_count) for i in left]
        return lax.ppermute(x, "lon", pairs + [(b, a) for a, b in pairs])

    lon_at = lax.axis_index("lon").astype(jnp.int32).reshape(1)
    second = lon_at[0] // 2 % 2
    first_column, last_column = cells[:1], cells[CX - 1 :]
    near0 = swap(tall, 0, 1)
    near1 = swap(tall, 1, 1)
    far0 = swap(jnp.where(second == 0, last_column, first_column), 0, 2)
    far1 = swap(jnp.where(second == 0, first_column, last_column), 1, 2)

    send, code = pl.pallas_call(
        slots_kernel,
        out_shape=(VMEM((3 * OWN * CAP, KP), BF16), VMEM((1, REC), jnp.int32)),
        in_specs=vmem(5),
        out_specs=tuple(vmem(2)),
        scratch_shapes=[VMEM((3 * KP, REC), F32), VMEM((3 * OWN * CAP, KP), F32)],
        name="slots",
    )(owner.reshape(1, REC), column.reshape(1, REC), w_t, iv_t, ob_t)
    recv = lax.all_to_all(
        send.reshape(OWN, 3, CAP, KP), owners, split_axis=0, concat_axis=0, tiled=True
    )
    recv = recv.reshape(3 * OWN * CAP, KP)

    own_mixes = pl.pallas_call(
        mixes_kernel,
        out_shape=VMEM((2, MIX, KP), BF16),
        in_specs=smem(1) + vmem(2),
        out_specs=vmem(1)[0],
        scratch_shapes=[VMEM((MIX, KP), F32)],
        name="mixes",
    )(pert_index, pert_table, member_mix)
    mixes = [own_mixes]
    for partner in ((1, 0, 3, 2), (3, 2, 1, 0), (2, 3, 0, 1)):
        mixes.append(lax.ppermute(own_mixes, "mem", list(enumerate(partner))))

    fields, back = pl.pallas_call(
        functools.partial(window_kernel, scale=1.0 / (OWN * REC * K)),
        out_shape=(VMEM((3, CX, K, CY), BF16), VMEM((OWN * CAP, KP), BF16)),
        in_specs=smem(2) + vmem(12),
        out_specs=tuple(vmem(2)),
        scratch_shapes=[
            VMEM((14, ROWS + 16, KP), F32),
            VMEM((RUNS, 14, ROWS + 16, KP), F32),
            VMEM((RUNS, 14, ROWS + 16, KP), F32),
            VMEM((14, ROWS, KP), F32),
            VMEM((16, KP), F32),
            VMEM((MEMBERS // 2, 2 * KP, 2 * KP), BF16),
            VMEM((2 * KP, 2 * KP), BF16),
            VMEM((KP, 2 * KP), BF16),
            VMEM((3 * OWN * CAP, KP), F32),
            VMEM((MEMBERS, OWN * CAP, KP), F32),
            VMEM((MEMBERS, OWN * CAP, KP), F32),
            VMEM((KP, KP), F32),
        ],
        name="window",
    )(
        mem, lon_at, near(tall), near(near0), near(near1), near(far0), near(far1), near(recv),
        *map(near, mixes),
        base_kh.reshape(1, K), base_mix,
    )

    returned = lax.all_to_all(
        back.reshape(OWN, CAP, KP), owners, split_axis=0, concat_axis=0, tiled=True
    )
    returned = returned.reshape(OWN * CAP, KP)
    misfit_t, gram, proj = pl.pallas_call(
        result_kernel,
        out_shape=(
            jax.ShapeDtypeStruct((K, REC), F32),
            jax.ShapeDtypeStruct((MEMBERS, MEMBERS), F32),
            jax.ShapeDtypeStruct((1, MEMBERS), F32),
        ),
        in_specs=vmem(4),
        out_specs=tuple(vmem(3)),
        name="result",
    )(near(returned), near(code), w_t, ob_t)
    proj = proj.reshape(MEMBERS)
    fields = jnp.transpose(fields, (0, 2, 1, 3))
    member_temp, base_temp = fields[:2], fields[2]

    return member_temp, base_temp, gram, proj, misfit_t.T


def solution(mesh):
    placed = (
        P(None, "lon", "lat"),
        P("lon", "lat"),
        P(),
        P("mem"),
        P(),
        P("mem", None, None),
        P(),
        P(("lat", "lon"), None),
        P(("lat", "lon")),
        P(("lat", "lon"), None),
        P(("lat", "lon"), None),
        P(("lat", "lon"), None),
    )
    return jax.shard_map(
        on_device,
        mesh=mesh,
        in_specs=placed,
        out_specs=(
            P("mem", None, "lon", "lat"),
            P(None, "lon", "lat"),
            P(),
            P(),
            P(("lat", "lon"), None),
        ),
        check_vma=False,
    )
```

```python
import functools

import jax
import jax.numpy as jnp
from jax import lax
from jax.experimental import pallas as pl
from jax.experimental.pallas import tpu as pltpu
from jax.sharding import PartitionSpec as P


STEPS = 5
BLOCKS = (4, 5, 4, 6, 4)
K = 100
KP = 128
SPARE = KP - K
CX = 4
CY = 128
CAP = 4
OWN = 128
REC = 256
HALO = 8
ROWS = CY + 2 * HALO
COLS = CX * CY
MEMBERS = 8
RUNS = MEMBERS + 1
MIX = 104
PAIRS = [(a, b) for a in range(MEMBERS) for b in range(a, MEMBERS)]
F32 = jnp.float32
BF16 = jnp.bfloat16
NT = (((1,), (1,)), ((), ()))
NN = (((1,), (0,)), ((), ()))
TN = (((0,), (0,)), ((), ()))
SMEM = pltpu.SMEM
VMEM = pltpu.VMEM


def dot(a, b, dims):
    return lax.dot_general(a, b, dims, preferred_element_type=F32)


def ones_where(cond):
    return jnp.where(cond, 1.0, 0.0).astype(BF16)


def iota(shape, dim):
    return lax.broadcasted_iota(jnp.int32, shape, dim)


def slots_kernel(owner_ref, column_ref, w_ref, iv_ref, ob_ref, out_ref, code_ref, pad, rows3):
    owner = owner_ref[...]
    column = column_ref[...]
    hit = iota((OWN, REC), 0) == owner
    before = ones_where(iota((REC, REC), 0) < iota((REC, REC), 1))
    earlier = dot(ones_where(hit), before, NN)
    rank = jnp.sum(jnp.where(hit, earlier, 0.0), 0, keepdims=True).astype(jnp.int32)
    slot = owner * CAP + rank
    code_ref[...] = slot
    pad[...] = jnp.zeros((3 * KP, REC), F32)
    for group, ref in enumerate((w_ref, iv_ref, ob_ref)):
        pad[group * KP : group * KP + K, :] = ref[...]
    pad[K : K + 1, :] = (column // CY + 1).astype(F32)
    pad[K + 1 : K + 2, :] = (column % CY).astype(F32)
    place = ones_where(iota((OWN * CAP, REC), 0) == slot)
    placed = dot(place, pad[...].astype(BF16), NT)
    for group in range(3):
        rows3[pl.ds(group, OWN * CAP, stride=3), :] = placed[:, group * KP : (group + 1) * KP]
    out_ref[...] = rows3[...].astype(BF16)


def mixes_kernel(index_ref, table_ref, mix_ref, out_ref, pad):
    for j in range(2):
        pad[...] = jnp.zeros((MIX, KP), F32)
        pad[0:K, 0:K] = mix_ref[j].astype(F32)
        kh = table_ref[pl.ds(index_ref[j], 1), :]
        high = kh.astype(BF16).astype(F32)
        pad[K : K + 1, 0:K] = high
        pad[K + 1 : K + 2, 0:K] = kh - high
        packed = pad[...].astype(BF16)
        for copy in range(4):
            out_ref[copy, j] = packed


def window_kernel(
    m_ref, lon_ref, own_ref, near0_ref, near1_ref, far0_ref, far1_ref, recv_ref,
    mixes_ref,
    base_kh_ref, base_mix_ref,
    fields_ref, out_ref,
    start, spread, ping, pong, ocean, kh_pad, mix_pad, one_pad, base_pad, slots, greens, weighted, sums,
    *, scale,
):
    body = pl.ds(8, ROWS)

    def fill(column, cells):
        cells = cells.astype(F32)
        start[column, body, :] = cells
        ocean[column] = jnp.broadcast_to(cells[:, K : K + 1], (ROWS, KP))

    near_side = 1 - lax.rem(lon_ref[0], 2)
    far_side = 1 - lax.rem(lon_ref[0] // 2, 2)
    start[13 * far_side, pl.ds(16, CY), :] = far0_ref[0].astype(F32)
    start[13 * (1 - far_side), pl.ds(16, CY), :] = far1_ref[0].astype(F32)
    for c in range(CX):
        fill(5 + c, own_ref[c])
        fill(1 + 8 * near_side + c, near0_ref[c])
        fill(1 + 8 * (1 - near_side) + c, near1_ref[c])
    kh_pad[...] = jnp.zeros((16, KP), F32)
    mix_pad[...] = jnp.zeros((MEMBERS // 2, 2 * KP, 2 * KP), BF16)
    for member in range(MEMBERS):
        pair, half = member // 2, member % 2
        spot = half * KP
        mix_pad[pair, spot : spot + K, spot : spot + KP] = mixes_ref[pair, half, 0:K, :]
        parts = mixes_ref[pair, half, MIX - 8 : MIX, :].astype(F32)
        kh_pad[member : member + 1, :] = parts[4:5] + parts[5:6]
    kh_pad[MEMBERS : MEMBERS + 1, 0:K] = base_kh_ref[...]
    same = iota((KP, KP), 0) == iota((KP, KP), 1)
    one_pad[...] = jnp.zeros((2 * KP, 2 * KP), BF16)
    one_pad[0:KP, 0:KP] = ones_where(same)
    one_pad[KP:, KP:] = ones_where(same)
    base_pad[...] = jnp.zeros((KP, 2 * KP), BF16)
    base_pad[0:K, 0:K] = base_mix_ref[...]
    base_pad[:, KP:] = ones_where(same)

    for c in range(1, 13):
        spread[c] = (start[c + 1, pl.ds(12, CY + 8), :] + start[c - 1, pl.ds(12, CY + 8), :]) + (
            start[c, pl.ds(13, CY + 8), :] + start[c, pl.ds(11, CY + 8), :]
        )

    for step in range(STEPS):
        source, target = ((ping, pong), (pong, ping))[step % 2]
        row0, count = (12, CY + 8) if step < STEPS - 1 else (16, CY)
        columns, block = 12 - 2 * step, BLOCKS[step]

        def at(run, lon, row, step=step, source=source, count=count):
            if step == 0:
                return start[lon, pl.ds(row, count), :]
            return source[run, lon, pl.ds(row, count), :]

        def rights(run, first, step=step, row0=row0, block=block, at=at):
            kh = kh_pad[pl.ds(run, 1), :]
            keep = 1.0 - 4.0 * kh
            parts = []
            for c in range(block):
                lon = first + c
                if step == 0:
                    around = spread[lon]
                else:
                    around = (at(run, lon + 1, row0) + at(run, lon - 1, row0)) + (
                        at(run, lon, row0 + 1) + at(run, lon, row0 - 1)
                    )
                parts.append(at(run, lon, row0) * keep + around * kh)
            return jnp.concatenate(parts, 0).astype(BF16)

        def put(run, first, mixed, row0=row0, count=count, block=block, at=at, target=target):
            for c in range(block):
                lon = first + c
                open_ = ocean[lon, pl.ds(row0 - 8, count), :] > 0.0
                new = jnp.where(open_, mixed[c * count : (c + 1) * count], at(run, lon, row0))
                target[run, lon, pl.ds(row0, count), :] = new.astype(BF16).astype(F32)

        def advance(pair, first, rights=rights, put=put):
            right = jnp.concatenate([rights(2 * pair, first), rights(2 * pair + 1, first)], 1)
            both = dot(right, mix_pad[pair], NT) + dot(right, one_pad[...], NT)
            put(2 * pair, first, both[:, :KP])
            put(2 * pair + 1, first, both[:, KP:])

        def advance_base(first, rights=rights, put=put):
            right = rights(MEMBERS, first)
            put(MEMBERS, first, dot(jnp.concatenate([right, right], 1), base_pad[...], NT))

        def turn(t, _, step=step, columns=columns, block=block, advance=advance, advance_base=advance_base):
            first = step + 1 + t * block
            for pair in range(MEMBERS // 2):
                advance(pair, first)
            advance_base(first)
            return 0

        if columns == block:
            turn(0, 0)
        else:
            lax.fori_loop(0, columns // block, turn, 0)

    final = pong

    def flat(run):
        return jnp.concatenate([final[run, 5 + c, pl.ds(16, CY), :].astype(BF16) for c in range(CX)], 0)

    for place, run in enumerate((2 * m_ref[0], 2 * m_ref[0] + 1, MEMBERS)):
        for c in range(CX):
            fields_ref[place, c] = final[run, 5 + c, pl.ds(16, CY), :].T[0:K, :].astype(BF16)

    count = OWN * CAP
    slots[...] = recv_ref[...].astype(F32)
    weight = slots[pl.ds(0, count, stride=3), :]
    inv_var = slots[pl.ds(1, count, stride=3), :]
    measured = slots[pl.ds(2, count, stride=3), :]
    at = ((weight[:, K : K + 1] - 1.0) * CY + weight[:, K + 1 : K + 2]).astype(jnp.int32)
    pick = ones_where(at == iota((count, COLS), 1))
    weight = jnp.where(iota((count, KP), 1) < K - 1, weight, 1.0)

    def model(x):
        below = pltpu.roll(x, KP - 1, 1)
        return below + weight * (x - below)

    base = dot(pick, flat(MEMBERS), NN)
    misfit = measured - model(base)
    for pair in range(MEMBERS // 2):
        both = dot(pick, jnp.concatenate([flat(2 * pair), flat(2 * pair + 1)], 1), NN)
        for half in range(2):
            green = model(both[:, half * KP : (half + 1) * KP] - base).astype(BF16).astype(F32)
            greens[2 * pair + half] = green
            weighted[2 * pair + half] = green * inv_var
    sums[...] = jnp.zeros((KP, KP), F32)
    for i, (a, b) in enumerate(PAIRS):
        sums[i : i + 1, :] = jnp.sum(weighted[a] * greens[b], 0, keepdims=True)
    for a in range(MEMBERS):
        sums[len(PAIRS) + a : len(PAIRS) + a + 1, :] = jnp.sum(weighted[a] * misfit, 0, keepdims=True)
    total = jnp.sum(sums[...].T, 0, keepdims=True) * scale
    high = jnp.broadcast_to(total.astype(BF16).astype(F32), (8, KP))
    rest = jnp.broadcast_to(total, (8, KP)) - high
    turn = iota((8, KP), 0) % CAP
    tail = jnp.where(
        turn == 0,
        pltpu.roll(high, K, 1),
        jnp.where(
            turn == 1,
            pltpu.roll(high, K - SPARE, 1),
            jnp.where(turn == 2, pltpu.roll(rest, K, 1), pltpu.roll(rest, K - SPARE, 1)),
        ),
    )
    rows = jnp.where(iota((1, 8, KP), 2) < K, base.reshape(count // 8, 8, KP), tail[None])
    out_ref[...] = rows.reshape(count, KP).astype(BF16)


def result_kernel(recv_ref, code_ref, w_ref, ob_ref, misfit_ref, gram_ref, proj_ref):
    recv = recv_ref[...]
    pick = ones_where(iota((OWN * CAP, REC), 0) == code_ref[...])
    picked = dot(recv, pick, TN)
    values = picked[0:K]
    deeper = jnp.concatenate([picked[1:K], picked[K - 1 : K]], 0)
    weight = w_ref[...]
    misfit_ref[...] = ob_ref[...] - (weight * values + (1.0 - weight) * deeper)
    part = jnp.sum(recv.astype(F32).reshape(OWN * CAP // 8, 8, KP), 0)
    part = part + pltpu.roll(part, 4, 0)
    part = part + pltpu.roll(part, 6, 0)
    sub, line = iota((8, KP), 0), iota((8, KP), 1)
    total = jnp.where(
        line < SPARE,
        pltpu.roll(jnp.broadcast_to(part[0:1], (8, KP)), SPARE, 1),
        pltpu.roll(jnp.broadcast_to(part[1:2], (8, KP)), 2 * SPARE, 1),
    )
    gram = jnp.zeros((8, KP), F32)
    for i, (a, b) in enumerate(PAIRS):
        here = ((sub == a) & (line == b)) | ((sub == b) & (line == a))
        gram = jnp.where(here, total[:, i : i + 1], gram)
    gram_ref[...] = gram[:, 0:MEMBERS]
    proj_ref[...] = pltpu.roll(total, KP - len(PAIRS), 1)[0:1, 0:MEMBERS]


def near(x):
    return pltpu.with_memory_space_constraint(x, VMEM)


def vmem(count):
    return [pl.BlockSpec(memory_space=VMEM)] * count


def smem(count):
    return [pl.BlockSpec(memory_space=SMEM)] * count


def on_device(
    initial_temp, land_mask, pert_table, pert_index, base_kh, member_mix, base_mix,
    owner, column, interp_w, obs_inv_var, observed,
):
    owners = ("lat", "lon")
    mem = lax.axis_index("mem").astype(jnp.int32).reshape(1)
    lat_at, lat_count = lax.axis_index("lat"), lax.axis_size("lat")
    lon_count = lax.axis_size("lon")
    w_t, iv_t, ob_t = interp_w.T, obs_inv_var.T, observed.T

    own_mixes = pl.pallas_call(
        mixes_kernel,
        out_shape=VMEM((4, 2, MIX, KP), BF16),
        in_specs=smem(1) + vmem(2),
        out_specs=vmem(1)[0],
        scratch_shapes=[VMEM((MIX, KP), F32)],
        name="mixes",
    )(pert_index, pert_table, member_mix)
    mixes = lax.all_to_all(own_mixes, "mem", split_axis=0, concat_axis=0, tiled=True)

    cells = jnp.transpose(initial_temp, (1, 2, 0)).astype(BF16)
    cells = jnp.concatenate(
        [
            cells,
            land_mask.astype(BF16)[:, :, None],
            jnp.zeros((CX, CY, KP - K - 1), BF16),
        ],
        2,
    )
    low, top = cells[:, :HALO], cells[:, CY - HALO :]
    even = lat_at % 2 == 0
    inner = [p for i in range(1, lat_count - 1, 2) for p in ((i, i + 1), (i + 1, i))]
    outer = [p for i in range(0, lat_count, 2) for p in ((i, i + 1), (i + 1, i))]
    at_inner = lax.ppermute(jnp.where(even, low, top), "lat", inner)
    at_outer = lax.ppermute(jnp.where(even, top, low), "lat", outer)
    at_inner = jnp.where(lat_at == 0, low[:, ::-1], at_inner)
    at_inner = jnp.where(lat_at == lat_count - 1, top[:, ::-1], at_inner)
    below, above = jnp.where(even, at_inner, at_outer), jnp.where(even, at_outer, at_inner)
    tall = jnp.concatenate([below, cells, above], 1)

    def swap(x, first, by):
        left = [i for i in range(lon_count) if (i // by) % 2 == first]
        pairs = [(i, (i + by) % lon_count) for i in left]
        return lax.ppermute(x, "lon", pairs + [(b, a) for a, b in pairs])

    lon_at = lax.axis_index("lon").astype(jnp.int32).reshape(1)
    second = lon_at[0] // 2 % 2
    first_column, last_column = cells[:1], cells[CX - 1 :]
    near0 = swap(tall, 0, 1)
    near1 = swap(tall, 1, 1)
    far0 = swap(jnp.where(second == 0, last_column, first_column), 0, 2)
    far1 = swap(jnp.where(second == 0, first_column, last_column), 1, 2)

    send, code = pl.pallas_call(
        slots_kernel,
        out_shape=(VMEM((3 * OWN * CAP, KP), BF16), VMEM((1, REC), jnp.int32)),
        in_specs=vmem(5),
        out_specs=tuple(vmem(2)),
        scratch_shapes=[VMEM((3 * KP, REC), F32), VMEM((3 * OWN * CAP, KP), F32)],
        name="slots",
    )(owner.reshape(1, REC), column.reshape(1, REC), w_t, iv_t, ob_t)
    recv = lax.all_to_all(
        send.reshape(OWN, 3, CAP, KP), owners, split_axis=0, concat_axis=0, tiled=True
    )
    recv = recv.reshape(3 * OWN * CAP, KP)

    fields, back = pl.pallas_call(
        functools.partial(window_kernel, scale=1.0 / (OWN * REC * K)),
        out_shape=(VMEM((3, CX, K, CY), BF16), VMEM((OWN * CAP, KP), BF16)),
        in_specs=smem(2) + vmem(9),
        out_specs=tuple(vmem(2)),
        scratch_shapes=[
            VMEM((14, ROWS + 16, KP), F32),
            VMEM((13, CY + 8, KP), F32),
            VMEM((RUNS, 14, ROWS + 16, KP), F32),
            VMEM((RUNS, 14, ROWS + 16, KP), F32),
            VMEM((14, ROWS, KP), F32),
            VMEM((16, KP), F32),
            VMEM((MEMBERS // 2, 2 * KP, 2 * KP), BF16),
            VMEM((2 * KP, 2 * KP), BF16),
            VMEM((KP, 2 * KP), BF16),
            VMEM((3 * OWN * CAP, KP), F32),
            VMEM((MEMBERS, OWN * CAP, KP), F32),
            VMEM((MEMBERS, OWN * CAP, KP), F32),
            VMEM((KP, KP), F32),
        ],
        name="window",
    )(
        mem, lon_at, near(tall), near(near0), near(near1), near(far0), near(far1), near(recv),
        near(mixes),
        base_kh.reshape(1, K), base_mix,
    )

    returned = lax.all_to_all(
        back.reshape(OWN, CAP, KP), owners, split_axis=0, concat_axis=0, tiled=True
    )
    returned = returned.reshape(OWN * CAP, KP)
    misfit_t, gram, proj = pl.pallas_call(
        result_kernel,
        out_shape=(
            jax.ShapeDtypeStruct((K, REC), F32),
            jax.ShapeDtypeStruct((MEMBERS, MEMBERS), F32),
            jax.ShapeDtypeStruct((1, MEMBERS), F32),
        ),
        in_specs=vmem(4),
        out_specs=tuple(vmem(3)),
        name="result",
    )(near(returned), near(code), w_t, ob_t)
    proj = proj.reshape(MEMBERS)
    fields = jnp.transpose(fields, (0, 2, 1, 3))
    member_temp, base_temp = fields[:2], fields[2]

    return member_temp, base_temp, gram, proj, misfit_t.T


def solution(mesh):
    placed = (
        P(None, "lon", "lat"),
        P("lon", "lat"),
        P(),
        P("mem"),
        P(),
        P("mem", None, None),
        P(),
        P(("lat", "lon"), None),
        P(("lat", "lon")),
        P(("lat", "lon"), None),
        P(("lat", "lon"), None),
        P(("lat", "lon"), None),
    )
    return jax.shard_map(
        on_device,
        mesh=mesh,
        in_specs=placed,
        out_specs=(
            P("mem", None, "lon", "lat"),
            P(None, "lon", "lat"),
            P(),
            P(),
            P(("lat", "lon"), None),
        ),
        check_vma=False,
    )
```

```python
import functools

import jax
import jax.numpy as jnp
from jax import lax
from jax.experimental import pallas as pl
from jax.experimental.pallas import tpu as pltpu
from jax.sharding import PartitionSpec as P


STEPS = 5
BLOCKS = (4, 5, 4, 6, 4)
K = 100
KP = 128
SPARE = KP - K
CX = 4
CY = 128
CAP = 4
OWN = 128
REC = 256
HALO = 8
ROWS = CY + 2 * HALO
COLS = CX * CY
MEMBERS = 8
RUNS = MEMBERS + 1
MIX = 104
PAIRS = [(a, b) for a in range(MEMBERS) for b in range(a, MEMBERS)]
F32 = jnp.float32
BF16 = jnp.bfloat16
NT = (((1,), (1,)), ((), ()))
NN = (((1,), (0,)), ((), ()))
TN = (((0,), (0,)), ((), ()))
SMEM = pltpu.SMEM
VMEM = pltpu.VMEM


def dot(a, b, dims):
    return lax.dot_general(a, b, dims, preferred_element_type=F32)


def ones_where(cond):
    return jnp.where(cond, 1.0, 0.0).astype(BF16)


def iota(shape, dim):
    return lax.broadcasted_iota(jnp.int32, shape, dim)


def slots_kernel(owner_ref, column_ref, w_ref, iv_ref, ob_ref, out_ref, code_ref, pad, rows3):
    owner = owner_ref[...]
    column = column_ref[...]
    hit = iota((OWN, REC), 0) == owner
    before = ones_where(iota((REC, REC), 0) < iota((REC, REC), 1))
    earlier = dot(ones_where(hit), before, NN)
    rank = jnp.sum(jnp.where(hit, earlier, 0.0), 0, keepdims=True).astype(jnp.int32)
    slot = owner * CAP + rank
    code_ref[...] = slot
    pad[...] = jnp.zeros((3 * KP, REC), F32)
    for group, ref in enumerate((w_ref, iv_ref, ob_ref)):
        pad[group * KP : group * KP + K, :] = ref[...]
    pad[K : K + 1, :] = (column // CY + 1).astype(F32)
    pad[K + 1 : K + 2, :] = (column % CY).astype(F32)
    place = ones_where(iota((OWN * CAP, REC), 0) == slot)
    placed = dot(place, pad[...].astype(BF16), NT)
    for group in range(3):
        rows3[pl.ds(group, OWN * CAP, stride=3), :] = placed[:, group * KP : (group + 1) * KP]
    out_ref[...] = rows3[...].astype(BF16)


def mixes_kernel(index_ref, table_ref, mix_ref, out_ref, pad):
    for j in range(2):
        pad[...] = jnp.zeros((MIX, KP), F32)
        pad[0:K, 0:K] = mix_ref[j].astype(F32)
        kh = table_ref[pl.ds(index_ref[j], 1), :]
        high = kh.astype(BF16).astype(F32)
        pad[K : K + 1, 0:K] = high
        pad[K + 1 : K + 2, 0:K] = kh - high
        packed = pad[...].astype(BF16)
        for copy in range(4):
            out_ref[copy, j] = packed


def cells_kernel(
    lat_ref, lon_ref, temp_ref, mask_ref,
    cells_ref, inner_ref, outer_ref, far0_ref, far1_ref, pad,
):
    even = lax.rem(lat_ref[0], 2) == 0
    second = lax.rem(lon_ref[0] // 2, 2) == 0
    pad[...] = jnp.zeros((KP, CY), F32)
    turned = []
    for c in range(CX):
        pad[0:K, :] = temp_ref[:, c, :]
        pad[K : K + 1, :] = mask_ref[c : c + 1, :].astype(F32)
        x = pad[...].T
        low, top = x[0:HALO], x[CY - HALO : CY]
        cells_ref[c] = x.astype(BF16)
        inner_ref[c] = jnp.where(even, low, top).astype(BF16)
        outer_ref[c] = jnp.where(even, top, low).astype(BF16)
        turned.append(x)
    far0_ref[0] = jnp.where(second, turned[-1], turned[0]).astype(BF16)
    far1_ref[0] = jnp.where(second, turned[0], turned[-1]).astype(BF16)


def window_kernel(
    m_ref, lon_ref, own_ref, near0_ref, near1_ref, far0_ref, far1_ref, recv_ref,
    mixes_ref,
    base_kh_ref, base_mix_ref,
    fields_ref, out_ref,
    start, spread, ping, pong, ocean, kh_pad, mix_pad, one_pad, base_pad, slots, greens, weighted, sums,
    *, scale,
):
    body = pl.ds(8, ROWS)

    def fill(column, cells):
        cells = cells.astype(F32)
        start[column, body, :] = cells
        ocean[column] = jnp.broadcast_to(cells[:, K : K + 1], (ROWS, KP))

    near_side = 1 - lax.rem(lon_ref[0], 2)
    far_side = 1 - lax.rem(lon_ref[0] // 2, 2)
    start[13 * far_side, pl.ds(16, CY), :] = far0_ref[0].astype(F32)
    start[13 * (1 - far_side), pl.ds(16, CY), :] = far1_ref[0].astype(F32)
    for c in range(CX):
        fill(5 + c, own_ref[c])
        fill(1 + 8 * near_side + c, near0_ref[c])
        fill(1 + 8 * (1 - near_side) + c, near1_ref[c])
    kh_pad[...] = jnp.zeros((16, KP), F32)
    mix_pad[...] = jnp.zeros((MEMBERS // 2, 2 * KP, 2 * KP), BF16)
    for member in range(MEMBERS):
        pair, half = member // 2, member % 2
        spot = half * KP
        mix_pad[pair, spot : spot + K, spot : spot + KP] = mixes_ref[pair, half, 0:K, :]
        parts = mixes_ref[pair, half, MIX - 8 : MIX, :].astype(F32)
        kh_pad[member : member + 1, :] = parts[4:5] + parts[5:6]
    kh_pad[MEMBERS : MEMBERS + 1, 0:K] = base_kh_ref[...]
    same = iota((KP, KP), 0) == iota((KP, KP), 1)
    one_pad[...] = jnp.zeros((2 * KP, 2 * KP), BF16)
    one_pad[0:KP, 0:KP] = ones_where(same)
    one_pad[KP:, KP:] = ones_where(same)
    base_pad[...] = jnp.zeros((KP, 2 * KP), BF16)
    base_pad[0:K, 0:K] = base_mix_ref[...]
    base_pad[:, KP:] = ones_where(same)

    for c in range(1, 13):
        spread[c] = (start[c + 1, pl.ds(12, CY + 8), :] + start[c - 1, pl.ds(12, CY + 8), :]) + (
            start[c, pl.ds(13, CY + 8), :] + start[c, pl.ds(11, CY + 8), :]
        )

    for step in range(STEPS):
        source, target = ((ping, pong), (pong, ping))[step % 2]
        row0, count = (12, CY + 8) if step < STEPS - 1 else (16, CY)
        columns, block = 12 - 2 * step, BLOCKS[step]

        def at(run, lon, row, step=step, source=source, count=count):
            if step == 0:
                return start[lon, pl.ds(row, count), :]
            return source[run, lon, pl.ds(row, count), :]

        def rights(run, first, step=step, row0=row0, block=block, at=at):
            kh = kh_pad[pl.ds(run, 1), :]
            keep = 1.0 - 4.0 * kh
            parts = []
            for c in range(block):
                lon = first + c
                if step == 0:
                    around = spread[lon]
                else:
                    around = (at(run, lon + 1, row0) + at(run, lon - 1, row0)) + (
                        at(run, lon, row0 + 1) + at(run, lon, row0 - 1)
                    )
                parts.append(at(run, lon, row0) * keep + around * kh)
            return jnp.concatenate(parts, 0).astype(BF16)

        def put(run, first, mixed, row0=row0, count=count, block=block, at=at, target=target):
            for c in range(block):
                lon = first + c
                open_ = ocean[lon, pl.ds(row0 - 8, count), :] > 0.0
                new = jnp.where(open_, mixed[c * count : (c + 1) * count], at(run, lon, row0))
                target[run, lon, pl.ds(row0, count), :] = new.astype(BF16).astype(F32)

        def advance(pair, first, rights=rights, put=put):
            right = jnp.concatenate([rights(2 * pair, first), rights(2 * pair + 1, first)], 1)
            both = dot(right, mix_pad[pair], NT) + dot(right, one_pad[...], NT)
            put(2 * pair, first, both[:, :KP])
            put(2 * pair + 1, first, both[:, KP:])

        def advance_base(first, rights=rights, put=put):
            right = rights(MEMBERS, first)
            put(MEMBERS, first, dot(jnp.concatenate([right, right], 1), base_pad[...], NT))

        def turn(t, _, step=step, columns=columns, block=block, advance=advance, advance_base=advance_base):
            first = step + 1 + t * block
            for pair in range(MEMBERS // 2):
                advance(pair, first)
            advance_base(first)
            return 0

        if columns == block:
            turn(0, 0)
        else:
            lax.fori_loop(0, columns // block, turn, 0)

    final = pong

    def flat(run):
        return jnp.concatenate([final[run, 5 + c, pl.ds(16, CY), :].astype(BF16) for c in range(CX)], 0)

    for place, run in enumerate((2 * m_ref[0], 2 * m_ref[0] + 1, MEMBERS)):
        for c in range(CX):
            fields_ref[place, c] = final[run, 5 + c, pl.ds(16, CY), :].T[0:K, :].astype(BF16)

    count = OWN * CAP
    slots[...] = recv_ref[...].astype(F32)
    weight = slots[pl.ds(0, count, stride=3), :]
    inv_var = slots[pl.ds(1, count, stride=3), :]
    measured = slots[pl.ds(2, count, stride=3), :]
    at = ((weight[:, K : K + 1] - 1.0) * CY + weight[:, K + 1 : K + 2]).astype(jnp.int32)
    pick = ones_where(at == iota((count, COLS), 1))
    weight = jnp.where(iota((count, KP), 1) < K - 1, weight, 1.0)

    def model(x):
        below = pltpu.roll(x, KP - 1, 1)
        return below + weight * (x - below)

    base = dot(pick, flat(MEMBERS), NN)
    misfit = measured - model(base)
    for pair in range(MEMBERS // 2):
        both = dot(pick, jnp.concatenate([flat(2 * pair), flat(2 * pair + 1)], 1), NN)
        for half in range(2):
            green = model(both[:, half * KP : (half + 1) * KP] - base).astype(BF16).astype(F32)
            greens[2 * pair + half] = green
            weighted[2 * pair + half] = green * inv_var
    sums[...] = jnp.zeros((KP, KP), F32)
    for i, (a, b) in enumerate(PAIRS):
        sums[i : i + 1, :] = jnp.sum(weighted[a] * greens[b], 0, keepdims=True)
    for a in range(MEMBERS):
        sums[len(PAIRS) + a : len(PAIRS) + a + 1, :] = jnp.sum(weighted[a] * misfit, 0, keepdims=True)
    total = jnp.sum(sums[...].T, 0, keepdims=True) * scale
    high = jnp.broadcast_to(total.astype(BF16).astype(F32), (8, KP))
    rest = jnp.broadcast_to(total, (8, KP)) - high
    turn = iota((8, KP), 0) % CAP
    tail = jnp.where(
        turn == 0,
        pltpu.roll(high, K, 1),
        jnp.where(
            turn == 1,
            pltpu.roll(high, K - SPARE, 1),
            jnp.where(turn == 2, pltpu.roll(rest, K, 1), pltpu.roll(rest, K - SPARE, 1)),
        ),
    )
    rows = jnp.where(iota((1, 8, KP), 2) < K, base.reshape(count // 8, 8, KP), tail[None])
    out_ref[...] = rows.reshape(count, KP).astype(BF16)


def result_kernel(recv_ref, code_ref, w_ref, ob_ref, misfit_ref, gram_ref, proj_ref):
    recv = recv_ref[...]
    pick = ones_where(iota((OWN * CAP, REC), 0) == code_ref[...])
    picked = dot(recv, pick, TN)
    values = picked[0:K]
    deeper = jnp.concatenate([picked[1:K], picked[K - 1 : K]], 0)
    weight = w_ref[...]
    misfit_ref[...] = ob_ref[...] - (weight * values + (1.0 - weight) * deeper)
    part = jnp.sum(recv.astype(F32).reshape(OWN * CAP // 8, 8, KP), 0)
    part = part + pltpu.roll(part, 4, 0)
    part = part + pltpu.roll(part, 6, 0)
    sub, line = iota((8, KP), 0), iota((8, KP), 1)
    total = jnp.where(
        line < SPARE,
        pltpu.roll(jnp.broadcast_to(part[0:1], (8, KP)), SPARE, 1),
        pltpu.roll(jnp.broadcast_to(part[1:2], (8, KP)), 2 * SPARE, 1),
    )
    gram = jnp.zeros((8, KP), F32)
    for i, (a, b) in enumerate(PAIRS):
        here = ((sub == a) & (line == b)) | ((sub == b) & (line == a))
        gram = jnp.where(here, total[:, i : i + 1], gram)
    gram_ref[...] = gram[:, 0:MEMBERS]
    proj_ref[...] = pltpu.roll(total, KP - len(PAIRS), 1)[0:1, 0:MEMBERS]


def near(x):
    return pltpu.with_memory_space_constraint(x, VMEM)


def vmem(count):
    return [pl.BlockSpec(memory_space=VMEM)] * count


def smem(count):
    return [pl.BlockSpec(memory_space=SMEM)] * count


def on_device(
    initial_temp, land_mask, pert_table, pert_index, base_kh, member_mix, base_mix,
    owner, column, interp_w, obs_inv_var, observed,
):
    owners = ("lat", "lon")
    mem = lax.axis_index("mem").astype(jnp.int32).reshape(1)
    lat_at, lat_count = lax.axis_index("lat"), lax.axis_size("lat")
    lon_count = lax.axis_size("lon")
    w_t, iv_t, ob_t = interp_w.T, obs_inv_var.T, observed.T

    own_mixes = pl.pallas_call(
        mixes_kernel,
        out_shape=VMEM((4, 2, MIX, KP), BF16),
        in_specs=smem(1) + vmem(2),
        out_specs=vmem(1)[0],
        scratch_shapes=[VMEM((MIX, KP), F32)],
        name="mixes",
    )(pert_index, pert_table, member_mix)
    mixes = lax.all_to_all(own_mixes, "mem", split_axis=0, concat_axis=0, tiled=True)

    lat_row = lat_at.astype(jnp.int32).reshape(1)
    lon_at = lax.axis_index("lon").astype(jnp.int32).reshape(1)
    cells, for_inner, for_outer, for_far0, for_far1 = pl.pallas_call(
        cells_kernel,
        out_shape=(
            VMEM((CX, CY, KP), BF16),
            VMEM((CX, HALO, KP), BF16),
            VMEM((CX, HALO, KP), BF16),
            VMEM((1, CY, KP), BF16),
            VMEM((1, CY, KP), BF16),
        ),
        in_specs=smem(2) + vmem(2),
        out_specs=tuple(vmem(5)),
        scratch_shapes=[VMEM((KP, CY), F32)],
        name="cells",
    )(lat_row, lon_at, near(initial_temp), near(land_mask))
    low, top = cells[:, :HALO], cells[:, CY - HALO :]
    even = lat_at % 2 == 0
    inner = [p for i in range(1, lat_count - 1, 2) for p in ((i, i + 1), (i + 1, i))]
    outer = [p for i in range(0, lat_count, 2) for p in ((i, i + 1), (i + 1, i))]
    at_inner = lax.ppermute(for_inner, "lat", inner)
    at_outer = lax.ppermute(for_outer, "lat", outer)
    at_inner = jnp.where(lat_at == 0, low[:, ::-1], at_inner)
    at_inner = jnp.where(lat_at == lat_count - 1, top[:, ::-1], at_inner)
    below, above = jnp.where(even, at_inner, at_outer), jnp.where(even, at_outer, at_inner)
    tall = jnp.concatenate([below, cells, above], 1)

    def swap(x, first, by):
        left = [i for i in range(lon_count) if (i // by) % 2 == first]
        pairs = [(i, (i + by) % lon_count) for i in left]
        return lax.ppermute(x, "lon", pairs + [(b, a) for a, b in pairs])

    near0 = swap(tall, 0, 1)
    near1 = swap(tall, 1, 1)
    far0 = swap(for_far0, 0, 2)
    far1 = swap(for_far1, 1, 2)

    send, code = pl.pallas_call(
        slots_kernel,
        out_shape=(VMEM((3 * OWN * CAP, KP), BF16), VMEM((1, REC), jnp.int32)),
        in_specs=vmem(5),
        out_specs=tuple(vmem(2)),
        scratch_shapes=[VMEM((3 * KP, REC), F32), VMEM((3 * OWN * CAP, KP), F32)],
        name="slots",
    )(owner.reshape(1, REC), column.reshape(1, REC), near(w_t), near(iv_t), near(ob_t))
    recv = lax.all_to_all(
        send.reshape(OWN, 3, CAP, KP), owners, split_axis=0, concat_axis=0, tiled=True
    )
    recv = recv.reshape(3 * OWN * CAP, KP)

    fields, back = pl.pallas_call(
        functools.partial(window_kernel, scale=1.0 / (OWN * REC * K)),
        out_shape=(VMEM((3, CX, K, CY), BF16), VMEM((OWN * CAP, KP), BF16)),
        in_specs=smem(2) + vmem(9),
        out_specs=tuple(vmem(2)),
        scratch_shapes=[
            VMEM((14, ROWS + 16, KP), F32),
            VMEM((13, CY + 8, KP), F32),
            VMEM((RUNS, 14, ROWS + 16, KP), F32),
            VMEM((RUNS, 14, ROWS + 16, KP), F32),
            VMEM((14, ROWS, KP), F32),
            VMEM((16, KP), F32),
            VMEM((MEMBERS // 2, 2 * KP, 2 * KP), BF16),
            VMEM((2 * KP, 2 * KP), BF16),
            VMEM((KP, 2 * KP), BF16),
            VMEM((3 * OWN * CAP, KP), F32),
            VMEM((MEMBERS, OWN * CAP, KP), F32),
            VMEM((MEMBERS, OWN * CAP, KP), F32),
            VMEM((KP, KP), F32),
        ],
        name="window",
    )(
        mem, lon_at, near(tall), near(near0), near(near1), near(far0), near(far1), near(recv),
        near(mixes),
        base_kh.reshape(1, K), base_mix,
    )

    returned = lax.all_to_all(
        back.reshape(OWN, CAP, KP), owners, split_axis=0, concat_axis=0, tiled=True
    )
    returned = returned.reshape(OWN * CAP, KP)
    misfit_t, gram, proj = pl.pallas_call(
        result_kernel,
        out_shape=(
            jax.ShapeDtypeStruct((K, REC), F32),
            jax.ShapeDtypeStruct((MEMBERS, MEMBERS), F32),
            jax.ShapeDtypeStruct((1, MEMBERS), F32),
        ),
        in_specs=vmem(4),
        out_specs=tuple(vmem(3)),
        name="result",
    )(near(returned), near(code), near(w_t), near(ob_t))
    proj = proj.reshape(MEMBERS)
    fields = jnp.transpose(fields, (0, 2, 1, 3))
    member_temp, base_temp = fields[:2], fields[2]

    return member_temp, base_temp, gram, proj, misfit_t.T


def solution(mesh):
    placed = (
        P(None, "lon", "lat"),
        P("lon", "lat"),
        P(),
        P("mem"),
        P(),
        P("mem", None, None),
        P(),
        P(("lat", "lon"), None),
        P(("lat", "lon")),
        P(("lat", "lon"), None),
        P(("lat", "lon"), None),
        P(("lat", "lon"), None),
    )
    return jax.shard_map(
        on_device,
        mesh=mesh,
        in_specs=placed,
        out_specs=(
            P("mem", None, "lon", "lat"),
            P(None, "lon", "lat"),
            P(),
            P(),
            P(("lat", "lon"), None),
        ),
        check_vma=False,
    )
```

```python
import functools

import jax
import jax.numpy as jnp
from jax import lax
from jax.experimental import pallas as pl
from jax.experimental.pallas import tpu as pltpu
from jax.sharding import PartitionSpec as P


STEPS = 5
BLOCKS = (4, 5, 4, 6, 4)
K = 100
KP = 128
SPARE = KP - K
CX = 4
CY = 128
CAP = 4
OWN = 128
REC = 256
HALO = 8
ROWS = CY + 2 * HALO
COLS = CX * CY
MEMBERS = 8
RUNS = MEMBERS + 1
MIX = 104
PAIRS = [(a, b) for a in range(MEMBERS) for b in range(a, MEMBERS)]
F32 = jnp.float32
BF16 = jnp.bfloat16
NT = (((1,), (1,)), ((), ()))
NN = (((1,), (0,)), ((), ()))
TN = (((0,), (0,)), ((), ()))
SMEM = pltpu.SMEM
VMEM = pltpu.VMEM


def dot(a, b, dims):
    return lax.dot_general(a, b, dims, preferred_element_type=F32)


def ones_where(cond):
    return jnp.where(cond, 1.0, 0.0).astype(BF16)


def iota(shape, dim):
    return lax.broadcasted_iota(jnp.int32, shape, dim)


def slots_kernel(owner_ref, column_ref, w_ref, iv_ref, ob_ref, out_ref, code_ref, pad, rows3):
    owner = owner_ref[...]
    column = column_ref[...]
    hit = iota((OWN, REC), 0) == owner
    before = ones_where(iota((REC, REC), 0) < iota((REC, REC), 1))
    earlier = dot(ones_where(hit), before, NN)
    rank = jnp.sum(jnp.where(hit, earlier, 0.0), 0, keepdims=True).astype(jnp.int32)
    slot = owner * CAP + rank
    code_ref[...] = slot
    pad[...] = jnp.zeros((3 * KP, REC), F32)
    for group, ref in enumerate((w_ref, iv_ref, ob_ref)):
        pad[group * KP : group * KP + K, :] = ref[...]
    pad[K : K + 1, :] = (column // CY + 1).astype(F32)
    pad[K + 1 : K + 2, :] = (column % CY).astype(F32)
    place = ones_where(iota((OWN * CAP, REC), 0) == slot)
    placed = dot(place, pad[...].astype(BF16), NT)
    for group in range(3):
        rows3[pl.ds(group, OWN * CAP, stride=3), :] = placed[:, group * KP : (group + 1) * KP]
    out_ref[...] = rows3[...].astype(BF16)


def mixes_kernel(index_ref, table_ref, mix_ref, out_ref, pad):
    pair = mix_ref[...].astype(F32)
    for j in range(2):
        pad[...] = jnp.zeros((MIX, KP), F32)
        pad[0:K, 0:K] = pair[:, j, :]
        kh = table_ref[pl.ds(index_ref[j], 1), :]
        high = kh.astype(BF16).astype(F32)
        pad[K : K + 1, 0:K] = high
        pad[K + 1 : K + 2, 0:K] = kh - high
        packed = pad[...].astype(BF16)
        for copy in range(4):
            out_ref[copy, j] = packed


def cells_kernel(
    lat_ref, lon_ref, temp_ref, mask_ref,
    cells_ref, inner_ref, outer_ref, far0_ref, far1_ref, pad,
):
    even = lax.rem(lat_ref[0], 2) == 0
    second = lax.rem(lon_ref[0] // 2, 2) == 0
    pad[...] = jnp.zeros((KP, CY), F32)
    turned = []
    for c in range(CX):
        pad[0:K, :] = temp_ref[:, c, :]
        pad[K : K + 1, :] = mask_ref[c : c + 1, :].astype(F32)
        x = pad[...].T
        low, top = x[0:HALO], x[CY - HALO : CY]
        cells_ref[c] = x.astype(BF16)
        inner_ref[c] = jnp.where(even, low, top).astype(BF16)
        outer_ref[c] = jnp.where(even, top, low).astype(BF16)
        turned.append(x)
    far0_ref[0] = jnp.where(second, turned[-1], turned[0]).astype(BF16)
    far1_ref[0] = jnp.where(second, turned[0], turned[-1]).astype(BF16)


def window_kernel(
    m_ref, lon_ref, own_ref, near0_ref, near1_ref, far0_ref, far1_ref, recv_ref,
    mixes_ref,
    base_kh_ref, base_mix_ref,
    fields_ref, out_ref,
    start, spread, ping, pong, ocean, kh_pad, mix_pad, one_pad, base_pad, slots, greens, weighted, sums,
    *, scale,
):
    body = pl.ds(8, ROWS)

    def fill(column, cells):
        cells = cells.astype(F32)
        start[column, body, :] = cells
        ocean[column] = jnp.broadcast_to(cells[:, K : K + 1], (ROWS, KP))

    near_side = 1 - lax.rem(lon_ref[0], 2)
    far_side = 1 - lax.rem(lon_ref[0] // 2, 2)
    start[13 * far_side, pl.ds(16, CY), :] = far0_ref[0].astype(F32)
    start[13 * (1 - far_side), pl.ds(16, CY), :] = far1_ref[0].astype(F32)
    for c in range(CX):
        fill(5 + c, own_ref[c])
        fill(1 + 8 * near_side + c, near0_ref[c])
        fill(1 + 8 * (1 - near_side) + c, near1_ref[c])
    kh_pad[...] = jnp.zeros((16, KP), F32)
    mix_pad[...] = jnp.zeros((MEMBERS // 2, 2 * KP, 2 * KP), BF16)
    for member in range(MEMBERS):
        pair, half = member // 2, member % 2
        spot = half * KP
        mix_pad[pair, spot : spot + K, spot : spot + KP] = mixes_ref[pair, half, 0:K, :]
        parts = mixes_ref[pair, half, MIX - 8 : MIX, :].astype(F32)
        kh_pad[member : member + 1, :] = parts[4:5] + parts[5:6]
    kh_pad[MEMBERS : MEMBERS + 1, 0:K] = base_kh_ref[...]
    same = iota((KP, KP), 0) == iota((KP, KP), 1)
    one_pad[...] = jnp.zeros((2 * KP, 2 * KP), BF16)
    one_pad[0:KP, 0:KP] = ones_where(same)
    one_pad[KP:, KP:] = ones_where(same)
    base_pad[...] = jnp.zeros((KP, 2 * KP), BF16)
    base_pad[0:K, 0:K] = base_mix_ref[...]
    base_pad[:, KP:] = ones_where(same)

    for c in range(1, 13):
        spread[c] = (start[c + 1, pl.ds(12, CY + 8), :] + start[c - 1, pl.ds(12, CY + 8), :]) + (
            start[c, pl.ds(13, CY + 8), :] + start[c, pl.ds(11, CY + 8), :]
        )

    for step in range(STEPS):
        source, target = ((ping, pong), (pong, ping))[step % 2]
        row0, count = (12, CY + 8) if step < STEPS - 1 else (16, CY)
        columns, block = 12 - 2 * step, BLOCKS[step]

        def at(run, lon, row, step=step, source=source, count=count):
            if step == 0:
                return start[lon, pl.ds(row, count), :]
            return source[run, lon, pl.ds(row, count), :]

        def rights(run, first, step=step, row0=row0, block=block, at=at):
            kh = kh_pad[pl.ds(run, 1), :]
            keep = 1.0 - 4.0 * kh
            parts = []
            for c in range(block):
                lon = first + c
                if step == 0:
                    around = spread[lon]
                else:
                    around = (at(run, lon + 1, row0) + at(run, lon - 1, row0)) + (
                        at(run, lon, row0 + 1) + at(run, lon, row0 - 1)
                    )
                parts.append(at(run, lon, row0) * keep + around * kh)
            return jnp.concatenate(parts, 0).astype(BF16)

        def put(run, first, mixed, row0=row0, count=count, block=block, at=at, target=target):
            for c in range(block):
                lon = first + c
                open_ = ocean[lon, pl.ds(row0 - 8, count), :] > 0.0
                new = jnp.where(open_, mixed[c * count : (c + 1) * count], at(run, lon, row0))
                target[run, lon, pl.ds(row0, count), :] = new.astype(BF16).astype(F32)

        def advance(pair, first, rights=rights, put=put):
            right = jnp.concatenate([rights(2 * pair, first), rights(2 * pair + 1, first)], 1)
            both = dot(right, mix_pad[pair], NT) + dot(right, one_pad[...], NT)
            put(2 * pair, first, both[:, :KP])
            put(2 * pair + 1, first, both[:, KP:])

        def advance_base(first, rights=rights, put=put):
            right = rights(MEMBERS, first)
            put(MEMBERS, first, dot(jnp.concatenate([right, right], 1), base_pad[...], NT))

        def turn(t, _, step=step, columns=columns, block=block, advance=advance, advance_base=advance_base):
            first = step + 1 + t * block
            for pair in range(MEMBERS // 2):
                advance(pair, first)
            advance_base(first)
            return 0

        if columns == block:
            turn(0, 0)
        else:
            lax.fori_loop(0, columns // block, turn, 0)

    final = pong

    def flat(run):
        return jnp.concatenate([final[run, 5 + c, pl.ds(16, CY), :].astype(BF16) for c in range(CX)], 0)

    for place, run in enumerate((2 * m_ref[0], 2 * m_ref[0] + 1, MEMBERS)):
        for c in range(CX):
            fields_ref[place, c] = final[run, 5 + c, pl.ds(16, CY), :].T[0:K, :].astype(BF16)

    count = OWN * CAP
    slots[...] = recv_ref[...].astype(F32)
    weight = slots[pl.ds(0, count, stride=3), :]
    inv_var = slots[pl.ds(1, count, stride=3), :]
    measured = slots[pl.ds(2, count, stride=3), :]
    at = ((weight[:, K : K + 1] - 1.0) * CY + weight[:, K + 1 : K + 2]).astype(jnp.int32)
    pick = ones_where(at == iota((count, COLS), 1))
    weight = jnp.where(iota((count, KP), 1) < K - 1, weight, 1.0)

    def model(x):
        below = pltpu.roll(x, KP - 1, 1)
        return below + weight * (x - below)

    base = dot(pick, flat(MEMBERS), NN)
    misfit = measured - model(base)
    for pair in range(MEMBERS // 2):
        both = dot(pick, jnp.concatenate([flat(2 * pair), flat(2 * pair + 1)], 1), NN)
        for half in range(2):
            green = model(both[:, half * KP : (half + 1) * KP] - base).astype(BF16).astype(F32)
            greens[2 * pair + half] = green
            weighted[2 * pair + half] = green * inv_var
    sums[...] = jnp.zeros((KP, KP), F32)
    for i, (a, b) in enumerate(PAIRS):
        sums[i : i + 1, :] = jnp.sum(weighted[a] * greens[b], 0, keepdims=True)
    for a in range(MEMBERS):
        sums[len(PAIRS) + a : len(PAIRS) + a + 1, :] = jnp.sum(weighted[a] * misfit, 0, keepdims=True)
    total = jnp.sum(sums[...].T, 0, keepdims=True) * scale
    high = jnp.broadcast_to(total.astype(BF16).astype(F32), (8, KP))
    rest = jnp.broadcast_to(total, (8, KP)) - high
    turn = iota((8, KP), 0) % CAP
    tail = jnp.where(
        turn == 0,
        pltpu.roll(high, K, 1),
        jnp.where(
            turn == 1,
            pltpu.roll(high, K - SPARE, 1),
            jnp.where(turn == 2, pltpu.roll(rest, K, 1), pltpu.roll(rest, K - SPARE, 1)),
        ),
    )
    rows = jnp.where(iota((1, 8, KP), 2) < K, base.reshape(count // 8, 8, KP), tail[None])
    out_ref[...] = rows.reshape(count, KP).astype(BF16)


def result_kernel(recv_ref, code_ref, w_ref, ob_ref, misfit_ref, gram_ref, proj_ref):
    recv = recv_ref[...]
    pick = ones_where(iota((OWN * CAP, REC), 0) == code_ref[...])
    picked = dot(recv, pick, TN)
    values = picked[0:K]
    deeper = jnp.concatenate([picked[1:K], picked[K - 1 : K]], 0)
    weight = w_ref[...]
    misfit_ref[...] = ob_ref[...] - (weight * values + (1.0 - weight) * deeper)
    part = jnp.sum(recv.astype(F32).reshape(OWN * CAP // 8, 8, KP), 0)
    part = part + pltpu.roll(part, 4, 0)
    part = part + pltpu.roll(part, 6, 0)
    sub, line = iota((8, KP), 0), iota((8, KP), 1)
    total = jnp.where(
        line < SPARE,
        pltpu.roll(jnp.broadcast_to(part[0:1], (8, KP)), SPARE, 1),
        pltpu.roll(jnp.broadcast_to(part[1:2], (8, KP)), 2 * SPARE, 1),
    )
    gram = jnp.zeros((8, KP), F32)
    for i, (a, b) in enumerate(PAIRS):
        here = ((sub == a) & (line == b)) | ((sub == b) & (line == a))
        gram = jnp.where(here, total[:, i : i + 1], gram)
    gram_ref[...] = gram[:, 0:MEMBERS]
    proj_ref[...] = pltpu.roll(total, KP - len(PAIRS), 1)[0:1, 0:MEMBERS]


def near(x):
    return pltpu.with_memory_space_constraint(x, VMEM)


def vmem(count):
    return [pl.BlockSpec(memory_space=VMEM)] * count


def smem(count):
    return [pl.BlockSpec(memory_space=SMEM)] * count


def on_device(
    initial_temp, land_mask, pert_table, pert_index, base_kh, member_mix, base_mix,
    owner, column, interp_w, obs_inv_var, observed,
):
    owners = ("lat", "lon")
    mem = lax.axis_index("mem").astype(jnp.int32).reshape(1)
    lat_at, lat_count = lax.axis_index("lat"), lax.axis_size("lat")
    lon_count = lax.axis_size("lon")
    w_t, iv_t, ob_t = interp_w.T, obs_inv_var.T, observed.T

    own_mixes = pl.pallas_call(
        mixes_kernel,
        out_shape=VMEM((4, 2, MIX, KP), BF16),
        in_specs=smem(1) + vmem(2),
        out_specs=vmem(1)[0],
        scratch_shapes=[VMEM((MIX, KP), F32)],
        name="mixes",
    )(pert_index, pert_table, jnp.transpose(member_mix, (1, 0, 2)))
    mixes = lax.all_to_all(own_mixes, "mem", split_axis=0, concat_axis=0, tiled=True)

    lat_row = lat_at.astype(jnp.int32).reshape(1)
    lon_at = lax.axis_index("lon").astype(jnp.int32).reshape(1)
    cells, for_inner, for_outer, for_far0, for_far1 = pl.pallas_call(
        cells_kernel,
        out_shape=(
            VMEM((CX, CY, KP), BF16),
            VMEM((CX, HALO, KP), BF16),
            VMEM((CX, HALO, KP), BF16),
            VMEM((1, CY, KP), BF16),
            VMEM((1, CY, KP), BF16),
        ),
        in_specs=smem(2) + vmem(2),
        out_specs=tuple(vmem(5)),
        scratch_shapes=[VMEM((KP, CY), F32)],
        name="cells",
    )(lat_row, lon_at, near(initial_temp), near(land_mask))
    low, top = cells[:, :HALO], cells[:, CY - HALO :]
    even = lat_at % 2 == 0
    inner = [p for i in range(1, lat_count - 1, 2) for p in ((i, i + 1), (i + 1, i))]
    outer = [p for i in range(0, lat_count, 2) for p in ((i, i + 1), (i + 1, i))]
    at_inner = lax.ppermute(for_inner, "lat", inner)
    at_outer = lax.ppermute(for_outer, "lat", outer)
    at_inner = jnp.where(lat_at == 0, low[:, ::-1], at_inner)
    at_inner = jnp.where(lat_at == lat_count - 1, top[:, ::-1], at_inner)
    below, above = jnp.where(even, at_inner, at_outer), jnp.where(even, at_outer, at_inner)
    tall = jnp.concatenate([below, cells, above], 1)

    def swap(x, first, by):
        left = [i for i in range(lon_count) if (i // by) % 2 == first]
        pairs = [(i, (i + by) % lon_count) for i in left]
        return lax.ppermute(x, "lon", pairs + [(b, a) for a, b in pairs])

    near0 = swap(tall, 0, 1)
    near1 = swap(tall, 1, 1)
    far0 = swap(for_far0, 0, 2)
    far1 = swap(for_far1, 1, 2)

    send, code = pl.pallas_call(
        slots_kernel,
        out_shape=(VMEM((3 * OWN * CAP, KP), BF16), VMEM((1, REC), jnp.int32)),
        in_specs=vmem(5),
        out_specs=tuple(vmem(2)),
        scratch_shapes=[VMEM((3 * KP, REC), F32), VMEM((3 * OWN * CAP, KP), F32)],
        name="slots",
    )(owner.reshape(1, REC), column.reshape(1, REC), near(w_t), near(iv_t), near(ob_t))
    recv = lax.all_to_all(
        send.reshape(OWN, 3, CAP, KP), owners, split_axis=0, concat_axis=0, tiled=True
    )
    recv = recv.reshape(3 * OWN * CAP, KP)

    fields, back = pl.pallas_call(
        functools.partial(window_kernel, scale=1.0 / (OWN * REC * K)),
        out_shape=(VMEM((3, CX, K, CY), BF16), VMEM((OWN * CAP, KP), BF16)),
        in_specs=smem(2) + vmem(9),
        out_specs=tuple(vmem(2)),
        scratch_shapes=[
            VMEM((14, ROWS + 16, KP), F32),
            VMEM((13, CY + 8, KP), F32),
            VMEM((RUNS, 14, ROWS + 16, KP), F32),
            VMEM((RUNS, 14, ROWS + 16, KP), F32),
            VMEM((14, ROWS, KP), F32),
            VMEM((16, KP), F32),
            VMEM((MEMBERS // 2, 2 * KP, 2 * KP), BF16),
            VMEM((2 * KP, 2 * KP), BF16),
            VMEM((KP, 2 * KP), BF16),
            VMEM((3 * OWN * CAP, KP), F32),
            VMEM((MEMBERS, OWN * CAP, KP), F32),
            VMEM((MEMBERS, OWN * CAP, KP), F32),
            VMEM((KP, KP), F32),
        ],
        name="window",
    )(
        mem, lon_at, near(tall), near(near0), near(near1), near(far0), near(far1), near(recv),
        near(mixes),
        base_kh.reshape(1, K), base_mix,
    )

    returned = lax.all_to_all(
        back.reshape(OWN, CAP, KP), owners, split_axis=0, concat_axis=0, tiled=True
    )
    returned = returned.reshape(OWN * CAP, KP)
    misfit_t, gram, proj = pl.pallas_call(
        result_kernel,
        out_shape=(
            jax.ShapeDtypeStruct((K, REC), F32),
            jax.ShapeDtypeStruct((MEMBERS, MEMBERS), F32),
            jax.ShapeDtypeStruct((1, MEMBERS), F32),
        ),
        in_specs=vmem(4),
        out_specs=tuple(vmem(3)),
        name="result",
    )(near(returned), near(code), near(w_t), near(ob_t))
    proj = proj.reshape(MEMBERS)
    fields = jnp.transpose(fields, (0, 2, 1, 3))
    member_temp, base_temp = fields[:2], fields[2]

    return member_temp, base_temp, gram, proj, misfit_t.T


def solution(mesh):
    placed = (
        P(None, "lon", "lat"),
        P("lon", "lat"),
        P(),
        P("mem"),
        P(),
        P("mem", None, None),
        P(),
        P(("lat", "lon"), None),
        P(("lat", "lon")),
        P(("lat", "lon"), None),
        P(("lat", "lon"), None),
        P(("lat", "lon"), None),
    )
    return jax.shard_map(
        on_device,
        mesh=mesh,
        in_specs=placed,
        out_specs=(
            P("mem", None, "lon", "lat"),
            P(None, "lon", "lat"),
            P(),
            P(),
            P(("lat", "lon"), None),
        ),
        check_vma=False,
    )
```
